256 devices in a mesh: row: 2 (over core), col: 64 (over z, y, x_hi), layer: 2 (over x_lo).
Axes of the slice: x: 4 (x_hi: 2, x_lo: 2; x = x_hi * 2 + x_lo), y: 4, z: 8, core: 2. Of those that a mesh axis runs over, the one named last changes fastest.
Arguments:
- flow_cols: int32 [16, 2, 64], P('row', 'layer', 'col'), may hold values from 0 to 64, as said below
- flow_vals: bfloat16 [16, 2, 64, 128, 128], P('row', 'layer', 'col'), may hold values from -22 to 22
- window_flow: bfloat16 [2, 8192, 32768], P('layer', 'row', 'col'), may hold values from -0.1403165 to 0.1403165
Outputs:
- flow_next: float32 [2048, 32768], P(('row', 'layer'), 'col')
The draws below stay inside these ranges and needn't reach their ends.
Inputs may be any that keep to these rules, and one draw needn't show every extreme that they name: `flow_cols`: an entry 64 marks an empty slot; the live entries of one block row and layer are distinct; every block row and layer has at least one live slot, and some block row and layer has all 64 slots live.
All inputs are finite; a program needn't handle non-finite values.
Results may differ from the reference program's by a relative error of at most 0.0003.
Values may be sent and summed in bfloat16 or wider, within the bound.
A program may use at most 128 MiB of HBM per device.

```python
import math
import jax
import jax.numpy as jnp
from jax import lax

BS = 128
KL = 64
NR = 16
NW = 256
SL = 64
N_LAYER = 2


def draw_flow_cols(key, part):
    scores = jax.random.randint(jax.random.fold_in(key, 11), (NR, N_LAYER, KL), 0, 1 << 20)
    ordering = jnp.argsort(scores * KL + jnp.arange(KL, dtype=jnp.int32), axis=-1, stable=True)
    chosen = ordering[:, :, :SL].astype(jnp.int32)
    counts = jax.random.randint(jax.random.fold_in(key, 12), (NR, N_LAYER, 1), 1, SL + 1)
    full_row = jax.random.randint(jax.random.fold_in(key, 13), (), 0, NR * N_LAYER)
    flat_index = jnp.arange(NR, dtype=jnp.int32)[:, None] * N_LAYER + jnp.arange(N_LAYER, dtype=jnp.int32)[None, :]
    counts = jnp.where(flat_index[:, :, None] == full_row, SL, counts)
    slot_scores = jax.random.randint(jax.random.fold_in(key, 14), (NR, N_LAYER, SL), 0, 1 << 20)
    slot_order = jnp.argsort(slot_scores * SL + jnp.arange(SL, dtype=jnp.int32), axis=-1, stable=True)
    slot_rank = jnp.argsort(slot_order, axis=-1, stable=True)
    return jnp.where(slot_rank < counts, chosen, KL).astype(jnp.int32)


def draw_flow_vals(key, part):
    shape = (NR, N_LAYER, SL, BS, BS)
    row_ramp = jnp.arange(NR * BS, dtype=jnp.float32) / max(NR * BS - 1, 1)
    spread = jax.random.uniform(jax.random.fold_in(key, 22), (NR * BS,), jnp.float32, 0.0, 1.0)
    base_draw = jnp.clip(jax.random.normal(jax.random.fold_in(key, 21), shape, jnp.float32), -4.0, 4.0)
    row_scale = jnp.exp(0.5 * math.log(3.0) * row_ramp + 0.5 * math.log(10.0) * spread)
    row_scale = row_scale.reshape(NR, 1, 1, BS, 1)
    return (base_draw * row_scale).astype(jnp.bfloat16)


def draw_window_flow(key, part):
    shape = (N_LAYER, KL * BS, NW * BS)
    weight_scale = 1.0 / math.sqrt(N_LAYER * SL * BS // 2)
    column_scale = jnp.exp(0.5 * math.log(10.0) * jax.random.uniform(jax.random.fold_in(key, 31), (NW * BS,), jnp.float32, 0.0, 1.0))
    base_draw = jnp.clip(jax.random.normal(jax.random.fold_in(key, 33), shape, jnp.float32), -4.0, 4.0)
    return (base_draw * column_scale[None, None, :] * weight_scale).astype(jnp.bfloat16)


def setup_inputs(seed: int = 0) -> dict:
    seeds = jax.random.split(jax.random.key(seed), 4)
    flow_cols = draw_flow_cols(jax.random.fold_in(seeds[3], 71), 0)
    flow_vals = draw_flow_vals(jax.random.fold_in(seeds[3], 71), 0)
    window_flow = draw_window_flow(jax.random.fold_in(seeds[3], 71), 0)
    return dict(flow_cols=flow_cols, flow_vals=flow_vals, window_flow=window_flow)


def reference(flow_cols, flow_vals, window_flow):
    window_blocks = window_flow.reshape(N_LAYER, KL, BS, NW * BS)

    def one_row(row_data):
        row_cols, row_vals = row_data

        def one_layer(running, layer_data):
            layer_blocks, layer_cols, layer_vals = layer_data
            slot_live = layer_cols < KL
            picked = jnp.take(layer_blocks, jnp.minimum(layer_cols, KL - 1).astype(jnp.int32), axis=0)
            masked = jnp.where(slot_live[:, None, None], layer_vals, jnp.zeros_like(layer_vals))
            product = jnp.einsum('sab,sbc->ac', masked.astype(jnp.float32), picked.astype(jnp.float32))
            return running + product, None

        start_value = jnp.zeros((BS, NW * BS), jnp.float32)
        running, unused = lax.scan(one_layer, start_value, (window_blocks, row_cols, row_vals))
        return running

    expanded = lax.map(one_row, (flow_cols, flow_vals)).reshape(NR * BS, NW * BS)
    squares = expanded * expanded
    column_mean = jnp.mean(squares, axis=0)
    return squares / (column_mean + 1e-6)
```

```python
import jax
import jax.numpy as jnp
from jax import lax
from jax.sharding import PartitionSpec as P


def body(flow_cols, flow_vals, window_flow):
    row = lax.axis_index("row")
    layer = lax.axis_index("layer")
    n_layer = lax.axis_size("layer")
    own_g = window_flow[0]
    half_rows = own_g.shape[0]
    other_g = lax.ppermute(own_g, "row", perm=[(0, 1), (1, 0)])
    panel = jnp.zeros((2 * half_rows, own_g.shape[1]), own_g.dtype)
    panel = lax.dynamic_update_slice_in_dim(panel, own_g, row * half_rows, 0)
    panel = lax.dynamic_update_slice_in_dim(panel, other_g, (1 - row) * half_rows, 0)

    block_size = flow_vals.shape[-1]
    block_count = panel.shape[0] // block_size
    row_blocks = flow_vals.shape[0]
    wide_cols = jnp.broadcast_to(flow_cols.astype(jnp.bfloat16)[..., None, None], flow_cols.shape + (16, 128))
    wide_cols = lax.optimization_barrier(wide_cols)
    slot_cols = lax.all_gather(wide_cols, "col", axis=2, tiled=True)[:, 0, :, 0, 0].astype(jnp.float32)
    slot_vals = lax.all_gather(flow_vals, "col", axis=2, tiled=True)[:, 0]
    column_ids = jnp.arange(block_count, dtype=jnp.float32)
    one_hot = (slot_cols[:, :, None] == column_ids[None, None, :]).astype(jnp.bfloat16)

    share = row_blocks // n_layer
    send_blocks = (1 - layer) * share
    keep_blocks = layer * share

    def expand(first_block):
        vals = lax.dynamic_slice_in_dim(slot_vals, first_block, share, 0)
        hot = lax.dynamic_slice_in_dim(one_hot, first_block, share, 0)
        dense = jnp.einsum("isab,isk->iakb", vals, hot, preferred_element_type=jnp.bfloat16)
        dense = dense.reshape(share * block_size, block_count * block_size)
        return jnp.dot(dense, panel, preferred_element_type=jnp.float32)

    sent = expand(send_blocks)
    received = lax.ppermute(sent, "layer", perm=[(0, 1), (1, 0)])
    summed = expand(keep_blocks) + received
    squares = summed * summed
    total_rows = row_blocks * block_size * lax.axis_size("row")
    column_sums = lax.psum(jnp.sum(squares, axis=0), ("row", "layer"))
    return squares / (column_sums / total_rows + 1e-06)


def solution(mesh):
    placed = (
        P("row", "layer", "col"),
        P("row", "layer", "col", None, None),
        P("layer", "row", "col"),
    )
    return jax.shard_map(
        body, mesh=mesh, in_specs=placed, out_specs=P(("row", "layer"), "col"), check_vma=False
    )
```

```python
import jax
import jax.numpy as jnp
from jax import lax
from jax.sharding import Mesh, PartitionSpec as P

COL_FACTORS = (8, 4, 2)
COL_PARTS = ("col_z", "col_y", "col_x")


def gather_slots(packed, split):
    if split:
        packed = lax.all_gather(packed, COL_PARTS[2], axis=0, tiled=True)
        return lax.all_gather(packed, COL_PARTS[:2], axis=0, tiled=True)
    return lax.all_gather(packed, "col", axis=0, tiled=True)


def body(flow_cols, flow_vals, window_flow, split):
    row = lax.axis_index("row")
    layer = lax.axis_index("layer")
    n_layer = lax.axis_size("layer")
    own_g = window_flow[0]
    half_rows = own_g.shape[0]
    other_g = lax.ppermute(own_g, "row", perm=[(0, 1), (1, 0)])
    panel = jnp.zeros((2 * half_rows, own_g.shape[1]), own_g.dtype)
    panel = lax.dynamic_update_slice_in_dim(panel, own_g, row * half_rows, 0)
    panel = lax.dynamic_update_slice_in_dim(panel, other_g, (1 - row) * half_rows, 0)

    block_size = flow_vals.shape[-1]
    block_count = panel.shape[0] // block_size
    row_blocks = flow_vals.shape[0]
    stacked = flow_vals.reshape(1, row_blocks * block_size, block_size)
    col_tile = jnp.zeros((1, 16, block_size), jnp.bfloat16)
    col_tile = col_tile.at[0, 0, :row_blocks].set(flow_cols.reshape(row_blocks).astype(jnp.bfloat16))
    packed = jnp.concatenate([stacked, col_tile], axis=1)
    gathered = gather_slots(packed, split)
    slot_count = gathered.shape[0]
    slot_vals = gathered[:, : row_blocks * block_size].reshape(slot_count, row_blocks, block_size, block_size)
    slot_cols = gathered[:, row_blocks * block_size, :row_blocks].astype(jnp.float32).T
    column_ids = jnp.arange(block_count, dtype=jnp.float32)
    one_hot = (slot_cols[:, :, None] == column_ids[None, None, :]).astype(jnp.bfloat16)

    share = row_blocks // n_layer
    send_blocks = (1 - layer) * share
    keep_blocks = layer * share

    def expand(first_block):
        vals = lax.dynamic_slice_in_dim(slot_vals, first_block, share, 1)
        hot = lax.dynamic_slice_in_dim(one_hot, first_block, share, 0)
        dense = jnp.einsum("siab,isk->iakb", vals, hot, preferred_element_type=jnp.bfloat16)
        dense = dense.reshape(share * block_size, block_count * block_size)
        return jnp.dot(dense, panel, preferred_element_type=jnp.float32)

    sent = expand(send_blocks)
    received = lax.ppermute(sent, "layer", perm=[(0, 1), (1, 0)])
    summed = expand(keep_blocks) + received
    squares = summed * summed
    total_rows = row_blocks * block_size * lax.axis_size("row")
    column_sums = lax.psum(jnp.sum(squares, axis=0), ("row", "layer"))
    return squares / (column_sums / total_rows + 1e-06)


def solution(mesh):
    split = mesh.shape["col"] == COL_FACTORS[0] * COL_FACTORS[1] * COL_FACTORS[2]
    if split:
        devices = mesh.devices.reshape(
            (mesh.shape["row"],) + COL_FACTORS + (mesh.shape["layer"],)
        )
        mesh = Mesh(devices, ("row",) + COL_PARTS + ("layer",))
        col = COL_PARTS
    else:
        col = "col"
    placed = (
        P("row", "layer", col),
        P("row", "layer", col, None, None),
        P("layer", "row", col),
    )
    return jax.shard_map(
        lambda c, v, w: body(c, v, w, split),
        mesh=mesh, in_specs=placed, out_specs=P(("row", "layer"), col), check_vma=False,
    )
```

```python
import jax
import jax.numpy as jnp
from jax.experimental import pallas as pl
from jax.experimental.pallas import tpu as pltpu
from jax import lax
from jax.sharding import Mesh, PartitionSpec as P


def sparse_rows_kernel(first_ref, cols_ref, vals_ref, panel_ref, out_ref, acc_ref):
    i = pl.program_id(0)
    block_row = first_ref[0] + i
    block_size = vals_ref.shape[-1]
    block_count = panel_ref.shape[0] // block_size
    acc_ref[...] = jnp.zeros_like(acc_ref)

    def step(s, carry):
        col = cols_ref[block_row, s]

        @pl.when(jnp.logical_and(col >= 0, col < block_count))
        def _():
            start = pl.multiple_of(col * block_size, block_size)
            acc_ref[...] += jnp.dot(
                vals_ref[s], panel_ref[pl.ds(start, block_size), :],
                preferred_element_type=jnp.float32,
            )

        return carry

    lax.fori_loop(0, vals_ref.shape[0], step, 0)
    out_ref[...] = acc_ref[...]


def sparse_rows(first, cols, gathered, panel, share):
    slot_count = gathered.shape[0]
    block_size = gathered.shape[-1]
    width = panel.shape[1]
    return pl.pallas_call(
        sparse_rows_kernel,
        out_shape=jax.ShapeDtypeStruct((share * block_size, width), jnp.float32),
        grid_spec=pltpu.PrefetchScalarGridSpec(
            num_scalar_prefetch=2,
            grid=(share,),
            in_specs=[
                pl.BlockSpec((slot_count, block_size, block_size), lambda i, f, c: (0, f[0] + i, 0)),
                pl.BlockSpec(panel.shape, lambda i, f, c: (0, 0), pipeline_mode=pl.Buffered(1)),
            ],
            out_specs=pl.BlockSpec((block_size, width), lambda i, f, c: (i, 0)),
            scratch_shapes=[pltpu.VMEM((block_size, width), jnp.float32)],
        ),
        compiler_params=pltpu.CompilerParams(vmem_limit_bytes=48 * 1024 * 1024),
        cost_estimate=pl.CostEstimate(
            flops=2 * share * slot_count * block_size * block_size * width,
            transcendentals=0,
            bytes_accessed=share * slot_count * block_size * block_size * 2 + panel.size * 2 + share * block_size * width * 4,
        ),
    )(first, cols, gathered, panel)

COL_FACTORS = (8, 4, 2)
COL_PARTS = ("col_z", "col_y", "col_x")


def gather_slots(packed, split):
    if split:
        packed = lax.all_gather(packed, COL_PARTS[2], axis=0, tiled=True)
        return lax.all_gather(packed, COL_PARTS[:2], axis=0, tiled=True)
    return lax.all_gather(packed, "col", axis=0, tiled=True)


def body(flow_cols, flow_vals, window_flow, split):
    row = lax.axis_index("row")
    layer = lax.axis_index("layer")
    n_layer = lax.axis_size("layer")
    own_g = window_flow[0]
    half_rows = own_g.shape[0]
    other_g = lax.ppermute(own_g, "row", perm=[(0, 1), (1, 0)])
    panel = jnp.zeros((2 * half_rows, own_g.shape[1]), own_g.dtype)
    panel = lax.dynamic_update_slice_in_dim(panel, own_g, row * half_rows, 0)
    panel = lax.dynamic_update_slice_in_dim(panel, other_g, (1 - row) * half_rows, 0)

    block_size = flow_vals.shape[-1]
    block_count = panel.shape[0] // block_size
    row_blocks = flow_vals.shape[0]
    stacked = flow_vals.reshape(1, row_blocks * block_size, block_size)
    col_tile = jnp.zeros((1, 16, block_size), jnp.bfloat16)
    col_tile = col_tile.at[0, 0, :row_blocks].set(flow_cols.reshape(row_blocks).astype(jnp.bfloat16))
    packed = jnp.concatenate([stacked, col_tile], axis=1)
    gathered = gather_slots(packed, split)
    slot_cols = gathered[:, row_blocks * block_size, :row_blocks].astype(jnp.int32).T

    share = row_blocks // n_layer
    send_first = ((1 - layer) * share).astype(jnp.int32).reshape(1)
    keep_first = (layer * share).astype(jnp.int32).reshape(1)

    def expand(first):
        return sparse_rows(first, slot_cols, gathered, panel, share)

    sent = expand(send_first)
    received = lax.ppermute(sent, "layer", perm=[(0, 1), (1, 0)])
    summed = expand(keep_first) + received
    squares = summed * summed
    total_rows = row_blocks * block_size * lax.axis_size("row")
    column_sums = lax.psum(jnp.sum(squares, axis=0), ("row", "layer"))
    return squares / (column_sums / total_rows + 1e-06)


def solution(mesh):
    split = mesh.shape["col"] == COL_FACTORS[0] * COL_FACTORS[1] * COL_FACTORS[2]
    if split:
        devices = mesh.devices.reshape(
            (mesh.shape["row"],) + COL_FACTORS + (mesh.shape["layer"],)
        )
        mesh = Mesh(devices, ("row",) + COL_PARTS + ("layer",))
        col = COL_PARTS
    else:
        col = "col"
    placed = (
        P("row", "layer", col),
        P("row", "layer", col, None, None),
        P("layer", "row", col),
    )
    return jax.shard_map(
        lambda c, v, w: body(c, v, w, split),
        mesh=mesh, in_specs=placed, out_specs=P(("row", "layer"), col), check_vma=False,
    )
```

```python
import jax
import jax.numpy as jnp
from jax.experimental import pallas as pl
from jax.experimental.pallas import tpu as pltpu
from jax import lax
from jax.sharding import Mesh, PartitionSpec as P


def dense_rows_kernel(first_ref, slot_of_ref, vals_ref, panel_ref, out_ref, stage_ref):
    block_size = vals_ref.shape[-1]
    share = vals_ref.shape[1] // block_size
    width = stage_ref.shape[1] // block_size
    chunks = panel_ref.shape[0] // stage_ref.shape[1]
    first = first_ref[0]
    out_ref[...] = jnp.zeros_like(out_ref)

    def chunk(j, carry):
        for i in range(share):
            for kk in range(width):
                slot = slot_of_ref[first + i, j * width + kk]
                rows = pl.ds(i * block_size, block_size)
                cols = pl.ds(kk * block_size, block_size)

                @pl.when(slot >= 0)
                def _():
                    stage_ref[rows, cols] = vals_ref[slot, rows, :]

                @pl.when(slot < 0)
                def _():
                    stage_ref[rows, cols] = jnp.zeros((block_size, block_size), stage_ref.dtype)

        start = pl.multiple_of(j * stage_ref.shape[1], stage_ref.shape[1])
        out_ref[...] += jnp.dot(
            stage_ref[...], panel_ref[pl.ds(start, stage_ref.shape[1]), :],
            preferred_element_type=jnp.float32,
        )
        return carry

    lax.fori_loop(0, chunks, chunk, 0)


def dense_rows(first, slot_of, gathered, panel, share, width=4):
    slot_count = gathered.shape[0]
    block_size = gathered.shape[-1]
    out_cols = panel.shape[1]
    return pl.pallas_call(
        dense_rows_kernel,
        out_shape=jax.ShapeDtypeStruct((share * block_size, out_cols), jnp.float32),
        grid_spec=pltpu.PrefetchScalarGridSpec(
            num_scalar_prefetch=2,
            grid=(1,),
            in_specs=[
                pl.BlockSpec((slot_count, share * block_size, block_size),
                             lambda i, f, t: (0, f[0] // share, 0), pipeline_mode=pl.Buffered(1)),
                pl.BlockSpec(panel.shape, lambda i, f, t: (0, 0), pipeline_mode=pl.Buffered(1)),
            ],
            out_specs=pl.BlockSpec((share * block_size, out_cols), lambda i, f, t: (0, 0)),
            scratch_shapes=[pltpu.VMEM((share * block_size, width * block_size), jnp.bfloat16)],
        ),
        compiler_params=pltpu.CompilerParams(vmem_limit_bytes=48 * 1024 * 1024),
        cost_estimate=pl.CostEstimate(
            flops=2 * share * block_size * panel.shape[0] * out_cols,
            transcendentals=0,
            bytes_accessed=slot_count * share * block_size * block_size * 2 + panel.size * 2 + share * block_size * out_cols * 4,
        ),
    )(first, slot_of, gathered, panel)


COL_FACTORS = (8, 4, 2)
COL_PARTS = ("col_z", "col_y", "col_x")


def gather_slots(packed, split):
    if split:
        packed = lax.all_gather(packed, COL_PARTS[2], axis=0, tiled=True)
        return lax.all_gather(packed, COL_PARTS[:2], axis=0, tiled=True)
    return lax.all_gather(packed, "col", axis=0, tiled=True)


def body(flow_cols, flow_vals, window_flow, split):
    row = lax.axis_index("row")
    layer = lax.axis_index("layer")
    n_layer = lax.axis_size("layer")
    own_g = window_flow[0]
    half_rows = own_g.shape[0]
    other_g = lax.ppermute(own_g, "row", perm=[(0, 1), (1, 0)])
    panel = jnp.zeros((2 * half_rows, own_g.shape[1]), own_g.dtype)
    panel = lax.dynamic_update_slice_in_dim(panel, own_g, row * half_rows, 0)
    panel = lax.dynamic_update_slice_in_dim(panel, other_g, (1 - row) * half_rows, 0)

    block_size = flow_vals.shape[-1]
    block_count = panel.shape[0] // block_size
    row_blocks = flow_vals.shape[0]
    stacked = flow_vals.reshape(1, row_blocks * block_size, block_size)
    col_tile = jnp.zeros((1, 16, block_size), jnp.bfloat16)
    col_tile = col_tile.at[0, 0, :row_blocks].set(flow_cols.reshape(row_blocks).astype(jnp.bfloat16))
    packed = jnp.concatenate([stacked, col_tile], axis=1)
    gathered = gather_slots(packed, split)
    slot_cols = gathered[:, row_blocks * block_size, :row_blocks].astype(jnp.int32).T
    slot_count = gathered.shape[0]
    hit = slot_cols[:, :, None] == jnp.arange(block_count, dtype=jnp.int32)[None, None, :]
    slot_ids = jnp.arange(slot_count, dtype=jnp.int32)[None, :, None]
    slot_of = jnp.max(jnp.where(hit, slot_ids, -1), axis=1)

    share = row_blocks // n_layer
    send_first = ((1 - layer) * share).astype(jnp.int32).reshape(1)
    keep_first = (layer * share).astype(jnp.int32).reshape(1)

    def expand(first):
        return dense_rows(first, slot_of, gathered, panel, share)

    sent = expand(send_first)
    received = lax.ppermute(sent, "layer", perm=[(0, 1), (1, 0)])
    summed = expand(keep_first) + received
    squares = summed * summed
    total_rows = row_blocks * block_size * lax.axis_size("row")
    column_sums = lax.psum(jnp.sum(squares, axis=0), ("row", "layer"))
    return squares / (column_sums / total_rows + 1e-06)


def solution(mesh):
    split = mesh.shape["col"] == COL_FACTORS[0] * COL_FACTORS[1] * COL_FACTORS[2]
    if split:
        devices = mesh.devices.reshape(
            (mesh.shape["row"],) + COL_FACTORS + (mesh.shape["layer"],)
        )
        mesh = Mesh(devices, ("row",) + COL_PARTS + ("layer",))
        col = COL_PARTS
    else:
        col = "col"
    placed = (
        P("row", "layer", col),
        P("row", "layer", col, None, None),
        P("layer", "row", col),
    )
    return jax.shard_map(
        lambda c, v, w: body(c, v, w, split),
        mesh=mesh, in_specs=placed, out_specs=P(("row", "layer"), col), check_vma=False,
    )
```

```python
import jax
import jax.numpy as jnp
from jax.experimental import pallas as pl
from jax.experimental.pallas import tpu as pltpu
from jax import lax
from jax.sharding import Mesh, PartitionSpec as P


def dense_rows_kernel(first_ref, slot_of_ref, vals_ref, panel_ref, out_ref, stage_ref):
    block_size = vals_ref.shape[-1]
    share = vals_ref.shape[1] // block_size
    width = stage_ref.shape[1] // block_size
    j = pl.program_id(0)
    first = first_ref[0]

    @pl.when(j == 0)
    def _():
        out_ref[...] = jnp.zeros_like(out_ref)

    for i in range(share):
        for kk in range(width):
            slot = slot_of_ref[first + i, j * width + kk]
            rows = pl.ds(i * block_size, block_size)
            block = vals_ref[jnp.maximum(slot, 0), rows, :]
            stage_ref[rows, pl.ds(kk * block_size, block_size)] = jnp.where(
                slot >= 0, block, jnp.zeros_like(block)
            )

    out_ref[...] += jnp.dot(stage_ref[...], panel_ref[...], preferred_element_type=jnp.float32)


def dense_rows(first, slot_of, gathered, panel, share, width=4):
    slot_count = gathered.shape[0]
    block_size = gathered.shape[-1]
    out_cols = panel.shape[1]
    return pl.pallas_call(
        dense_rows_kernel,
        out_shape=jax.ShapeDtypeStruct((share * block_size, out_cols), jnp.float32),
        grid_spec=pltpu.PrefetchScalarGridSpec(
            num_scalar_prefetch=2,
            grid=(panel.shape[0] // (width * block_size),),
            in_specs=[
                pl.BlockSpec((slot_count, share * block_size, block_size),
                             lambda j, f, t: (0, f[0] // share, 0), pipeline_mode=pl.Buffered(1)),
                pl.BlockSpec((width * block_size, out_cols), lambda j, f, t: (j, 0)),
            ],
            out_specs=pl.BlockSpec((share * block_size, out_cols), lambda j, f, t: (0, 0)),
            scratch_shapes=[pltpu.VMEM((share * block_size, width * block_size), jnp.bfloat16)],
        ),
        compiler_params=pltpu.CompilerParams(vmem_limit_bytes=48 * 1024 * 1024),
        cost_estimate=pl.CostEstimate(
            flops=2 * share * block_size * panel.shape[0] * out_cols,
            transcendentals=0,
            bytes_accessed=slot_count * share * block_size * block_size * 2 + panel.size * 2 + share * block_size * out_cols * 4,
        ),
    )(first, slot_of, gathered, panel)


COL_FACTORS = (8, 4, 2)
COL_PARTS = ("col_z", "col_y", "col_x")


def gather_slots(packed, split):
    if split:
        packed = lax.all_gather(packed, COL_PARTS[2], axis=0, tiled=True)
        return lax.all_gather(packed, COL_PARTS[:2], axis=0, tiled=True)
    return lax.all_gather(packed, "col", axis=0, tiled=True)


def body(flow_cols, flow_vals, window_flow, split):
    row = lax.axis_index("row")
    layer = lax.axis_index("layer")
    n_layer = lax.axis_size("layer")
    own_g = window_flow[0]
    half_rows = own_g.shape[0]
    other_g = lax.ppermute(own_g, "row", perm=[(0, 1), (1, 0)])
    panel = jnp.zeros((2 * half_rows, own_g.shape[1]), own_g.dtype)
    panel = lax.dynamic_update_slice_in_dim(panel, own_g, row * half_rows, 0)
    panel = lax.dynamic_update_slice_in_dim(panel, other_g, (1 - row) * half_rows, 0)

    block_size = flow_vals.shape[-1]
    block_count = panel.shape[0] // block_size
    row_blocks = flow_vals.shape[0]
    stacked = flow_vals.reshape(1, row_blocks * block_size, block_size)
    col_tile = jnp.zeros((1, 16, block_size), jnp.bfloat16)
    col_tile = col_tile.at[0, 0, :row_blocks].set(flow_cols.reshape(row_blocks).astype(jnp.bfloat16))
    packed = jnp.concatenate([stacked, col_tile], axis=1)
    gathered = gather_slots(packed, split)
    slot_cols = gathered[:, row_blocks * block_size, :row_blocks].astype(jnp.int32).T
    slot_count = gathered.shape[0]
    hit = slot_cols[:, :, None] == jnp.arange(block_count, dtype=jnp.int32)[None, None, :]
    slot_ids = jnp.arange(slot_count, dtype=jnp.int32)[None, :, None]
    slot_of = jnp.max(jnp.where(hit, slot_ids, -1), axis=1)

    share = row_blocks // n_layer
    send_first = ((1 - layer) * share).astype(jnp.int32).reshape(1)
    keep_first = (layer * share).astype(jnp.int32).reshape(1)

    def expand(first):
        return dense_rows(first, slot_of, gathered, panel, share)

    sent = expand(send_first)
    received = lax.ppermute(sent, "layer", perm=[(0, 1), (1, 0)])
    summed = expand(keep_first) + received
    squares = summed * summed
    total_rows = row_blocks * block_size * lax.axis_size("row")
    column_sums = lax.psum(jnp.sum(squares, axis=0), ("row", "layer"))
    return squares / (column_sums / total_rows + 1e-06)


def solution(mesh):
    split = mesh.shape["col"] == COL_FACTORS[0] * COL_FACTORS[1] * COL_FACTORS[2]
    if split:
        devices = mesh.devices.reshape(
            (mesh.shape["row"],) + COL_FACTORS + (mesh.shape["layer"],)
        )
        mesh = Mesh(devices, ("row",) + COL_PARTS + ("layer",))
        col = COL_PARTS
    else:
        col = "col"
    placed = (
        P("row", "layer", col),
        P("row", "layer", col, None, None),
        P("layer", "row", col),
    )
    return jax.shard_map(
        lambda c, v, w: body(c, v, w, split),
        mesh=mesh, in_specs=placed, out_specs=P(("row", "layer"), col), check_vma=False,
    )
```

```python
import jax
import jax.numpy as jnp
from jax.experimental import pallas as pl
from jax.experimental.pallas import tpu as pltpu
from jax import lax
from jax.sharding import Mesh, PartitionSpec as P


def dense_rows_kernel(first_ref, slot_of_ref, vals_ref, panel_ref, out_ref, stage_ref):
    block_size = vals_ref.shape[-1]
    share = vals_ref.shape[1] // block_size
    width = stage_ref.shape[1] // block_size
    j = pl.program_id(0)
    first = first_ref[0]

    @pl.when(j == 0)
    def _():
        out_ref[...] = jnp.zeros_like(out_ref)

    for i in range(share):
        for kk in range(width):
            slot = slot_of_ref[first + i, j * width + kk]
            rows = pl.ds(i * block_size, block_size)
            block = vals_ref[jnp.maximum(slot, 0), rows, :]
            stage_ref[rows, pl.ds(kk * block_size, block_size)] = jnp.where(
                slot >= 0, block, jnp.zeros_like(block)
            )

    out_ref[...] += jnp.dot(stage_ref[...], panel_ref[...], preferred_element_type=jnp.float32)


def dense_rows(first, slot_of, gathered, panel, share, width=4):
    slot_count = gathered.shape[0]
    block_size = gathered.shape[-1]
    out_cols = panel.shape[1]
    return pl.pallas_call(
        dense_rows_kernel,
        out_shape=jax.ShapeDtypeStruct((share * block_size, out_cols), jnp.float32),
        grid_spec=pltpu.PrefetchScalarGridSpec(
            num_scalar_prefetch=2,
            grid=(panel.shape[0] // (width * block_size),),
            in_specs=[
                pl.BlockSpec((slot_count, share * block_size, block_size),
                             lambda j, f, t: (0, f[0] // share, 0), pipeline_mode=pl.Buffered(1)),
                pl.BlockSpec((width * block_size, out_cols), lambda j, f, t: (j, 0)),
            ],
            out_specs=pl.BlockSpec((share * block_size, out_cols), lambda j, f, t: (0, 0)),
            scratch_shapes=[pltpu.VMEM((share * block_size, width * block_size), jnp.bfloat16)],
        ),
        compiler_params=pltpu.CompilerParams(vmem_limit_bytes=48 * 1024 * 1024),
        cost_estimate=pl.CostEstimate(
            flops=2 * share * block_size * panel.shape[0] * out_cols,
            transcendentals=0,
            bytes_accessed=slot_count * share * block_size * block_size * 2 + panel.size * 2 + share * block_size * out_cols * 4,
        ),
    )(first, slot_of, gathered, panel)


COL_FACTORS = (8, 4, 2)
COL_PARTS = ("col_z", "col_y", "col_x")


def gather_slots(packed, split):
    if split:
        partner = lax.ppermute(packed, COL_PARTS[2], perm=[(0, 1), (1, 0)])
        packed = jnp.concatenate([packed, partner], axis=0)
        return lax.all_gather(packed, COL_PARTS[:2], axis=0, tiled=True)
    return lax.all_gather(packed, "col", axis=0, tiled=True)


def body(flow_cols, flow_vals, window_flow, split):
    row = lax.axis_index("row")
    layer = lax.axis_index("layer")
    n_layer = lax.axis_size("layer")
    own_g = window_flow[0]
    half_rows = own_g.shape[0]
    other_g = lax.ppermute(own_g, "row", perm=[(0, 1), (1, 0)])
    panel = jnp.zeros((2 * half_rows, own_g.shape[1]), own_g.dtype)
    panel = lax.dynamic_update_slice_in_dim(panel, own_g, row * half_rows, 0)
    panel = lax.dynamic_update_slice_in_dim(panel, other_g, (1 - row) * half_rows, 0)

    block_size = flow_vals.shape[-1]
    block_count = panel.shape[0] // block_size
    row_blocks = flow_vals.shape[0]
    stacked = flow_vals.reshape(1, row_blocks * block_size, block_size)
    col_tile = jnp.zeros((1, 16, block_size), jnp.bfloat16)
    col_tile = col_tile.at[0, 0, :row_blocks].set(flow_cols.reshape(row_blocks).astype(jnp.bfloat16))
    packed = jnp.concatenate([stacked, col_tile], axis=1)
    gathered = gather_slots(packed, split)
    slot_cols = gathered[:, row_blocks * block_size, :row_blocks].astype(jnp.int32).T
    slot_count = gathered.shape[0]
    hit = slot_cols[:, :, None] == jnp.arange(block_count, dtype=jnp.int32)[None, None, :]
    slot_ids = jnp.arange(slot_count, dtype=jnp.int32)[None, :, None]
    slot_of = jnp.max(jnp.where(hit, slot_ids, -1), axis=1)

    share = row_blocks // n_layer
    send_first = ((1 - layer) * share).astype(jnp.int32).reshape(1)
    keep_first = (layer * share).astype(jnp.int32).reshape(1)

    piece = share // 2
    received = []
    for part in range(2):
        sent = dense_rows(send_first + part * piece, slot_of, gathered, panel, piece)
        received.append(lax.ppermute(sent, "layer", perm=[(0, 1), (1, 0)]))
    summed = dense_rows(keep_first, slot_of, gathered, panel, share) + jnp.concatenate(received, axis=0)
    squares = summed * summed
    total_rows = row_blocks * block_size * lax.axis_size("row")
    column_sums = lax.psum(jnp.sum(squares, axis=0), ("row", "layer"))
    return squares / (column_sums / total_rows + 1e-06)


def solution(mesh):
    split = mesh.shape["col"] == COL_FACTORS[0] * COL_FACTORS[1] * COL_FACTORS[2]
    if split:
        devices = mesh.devices.reshape(
            (mesh.shape["row"],) + COL_FACTORS + (mesh.shape["layer"],)
        )
        mesh = Mesh(devices, ("row",) + COL_PARTS + ("layer",))
        col = COL_PARTS
    else:
        col = "col"
    placed = (
        P("row", "layer", col),
        P("row", "layer", col, None, None),
        P("layer", "row", col),
    )
    return jax.shard_map(
        lambda c, v, w: body(c, v, w, split),
        mesh=mesh, in_specs=placed, out_specs=P(("row", "layer"), col), check_vma=False,
    )
```

```python
import jax
import jax.numpy as jnp
from jax.experimental import pallas as pl
from jax.experimental.pallas import tpu as pltpu
from jax import lax
from jax.sharding import Mesh, PartitionSpec as P


def dense_rows_kernel(first_ref, slot_of_ref, vals_ref, panel_ref, out_ref, stage_ref):
    block_size = vals_ref.shape[-1]
    share = vals_ref.shape[1] // block_size
    width = stage_ref.shape[1] // block_size
    j = pl.program_id(0)
    first = first_ref[0]

    @pl.when(j == 0)
    def _():
        out_ref[...] = jnp.zeros_like(out_ref)

    for i in range(share):
        for kk in range(width):
            slot = slot_of_ref[first + i, j * width + kk]
            rows = pl.ds(i * block_size, block_size)
            block = vals_ref[jnp.maximum(slot, 0), rows, :]
            stage_ref[rows, pl.ds(kk * block_size, block_size)] = jnp.where(
                slot >= 0, block, jnp.zeros_like(block)
            )

    out_ref[...] += jnp.dot(stage_ref[...], panel_ref[...], preferred_element_type=jnp.float32)


def dense_rows(first, slot_of, gathered, panel, share, width=8):
    slot_count = gathered.shape[0]
    block_size = gathered.shape[-1]
    out_cols = panel.shape[1]
    return pl.pallas_call(
        dense_rows_kernel,
        out_shape=jax.ShapeDtypeStruct((share * block_size, out_cols), jnp.float32),
        grid_spec=pltpu.PrefetchScalarGridSpec(
            num_scalar_prefetch=2,
            grid=(panel.shape[0] // (width * block_size),),
            in_specs=[
                pl.BlockSpec((slot_count, share * block_size, block_size),
                             lambda j, f, t: (0, f[0] // share, 0), pipeline_mode=pl.Buffered(1)),
                pl.BlockSpec((width * block_size, out_cols), lambda j, f, t: (j, 0)),
            ],
            out_specs=pl.BlockSpec((share * block_size, out_cols), lambda j, f, t: (0, 0)),
            scratch_shapes=[pltpu.VMEM((share * block_size, width * block_size), jnp.bfloat16)],
        ),
        compiler_params=pltpu.CompilerParams(vmem_limit_bytes=48 * 1024 * 1024),
        cost_estimate=pl.CostEstimate(
            flops=2 * share * block_size * panel.shape[0] * out_cols,
            transcendentals=0,
            bytes_accessed=slot_count * share * block_size * block_size * 2 + panel.size * 2 + share * block_size * out_cols * 4,
        ),
    )(first, slot_of, gathered, panel)


COL_FACTORS = (8, 4, 2)
COL_PARTS = ("col_z", "col_y", "col_x")


def gather_slots(packed, split):
    if split:
        packed = lax.all_gather(packed, COL_PARTS[2], axis=0, tiled=True)
        return lax.all_gather(packed, COL_PARTS[:2], axis=0, tiled=True)
    return lax.all_gather(packed, "col", axis=0, tiled=True)


def body(flow_cols, flow_vals, window_flow, split):
    row = lax.axis_index("row")
    layer = lax.axis_index("layer")
    n_layer = lax.axis_size("layer")
    own_g = window_flow[0]
    half_rows = own_g.shape[0]
    other_g = lax.ppermute(own_g, "row", perm=[(0, 1), (1, 0)])
    panel = jnp.zeros((2 * half_rows, own_g.shape[1]), own_g.dtype)
    panel = lax.dynamic_update_slice_in_dim(panel, own_g, row * half_rows, 0)
    panel = lax.dynamic_update_slice_in_dim(panel, other_g, (1 - row) * half_rows, 0)

    block_size = flow_vals.shape[-1]
    block_count = panel.shape[0] // block_size
    row_blocks = flow_vals.shape[0]
    stacked = flow_vals.reshape(1, row_blocks * block_size, block_size)
    col_tile = jnp.zeros((1, 16, block_size), jnp.bfloat16)
    col_tile = col_tile.at[0, 0, :row_blocks].set(flow_cols.reshape(row_blocks).astype(jnp.bfloat16))
    packed = jnp.concatenate([stacked, col_tile], axis=1)
    gathered = gather_slots(packed, split)
    slot_cols = gathered[:, row_blocks * block_size, :row_blocks].astype(jnp.int32).T
    slot_count = gathered.shape[0]
    hit = slot_cols[:, :, None] == jnp.arange(block_count, dtype=jnp.int32)[None, None, :]
    slot_ids = jnp.arange(slot_count, dtype=jnp.int32)[None, :, None]
    slot_of = jnp.max(jnp.where(hit, slot_ids, -1), axis=1)

    share = row_blocks // n_layer
    send_first = ((1 - layer) * share).astype(jnp.int32).reshape(1)
    keep_first = (layer * share).astype(jnp.int32).reshape(1)

    def expand(first):
        return dense_rows(first, slot_of, gathered, panel, share)

    sent = expand(send_first)
    received = lax.ppermute(sent, "layer", perm=[(0, 1), (1, 0)])
    summed = expand(keep_first) + received
    squares = summed * summed
    total_rows = row_blocks * block_size * lax.axis_size("row")
    column_sums = lax.psum(jnp.sum(squares, axis=0), ("row", "layer"))
    return squares / (column_sums / total_rows + 1e-06)


def solution(mesh):
    split = mesh.shape["col"] == COL_FACTORS[0] * COL_FACTORS[1] * COL_FACTORS[2]
    if split:
        devices = mesh.devices.reshape(
            (mesh.shape["row"],) + COL_FACTORS + (mesh.shape["layer"],)
        )
        mesh = Mesh(devices, ("row",) + COL_PARTS + ("layer",))
        col = COL_PARTS
    else:
        col = "col"
    placed = (
        P("row", "layer", col),
        P("row", "layer", col, None, None),
        P("layer", "row", col),
    )
    return jax.shard_map(
        lambda c, v, w: body(c, v, w, split),
        mesh=mesh, in_specs=placed, out_specs=P(("row", "layer"), col), check_vma=False,
    )
```

```python
import jax
import jax.numpy as jnp
from jax.experimental import pallas as pl
from jax.experimental.pallas import tpu as pltpu
from jax import lax
from jax.sharding import Mesh, PartitionSpec as P


def dense_rows_kernel(first_ref, slot_of_ref, vals_ref, panel_ref, out_ref, stage_ref):
    block_size = vals_ref.shape[-1]
    share = vals_ref.shape[1] // block_size
    width = stage_ref.shape[1] // block_size
    j = pl.program_id(0)
    first = first_ref[0]

    @pl.when(j == 0)
    def _():
        out_ref[...] = jnp.zeros_like(out_ref)

    for i in range(share):
        for kk in range(width):
            slot = slot_of_ref[first + i, j * width + kk]
            rows = pl.ds(i * block_size, block_size)
            block = vals_ref[jnp.maximum(slot, 0), rows, :]
            stage_ref[rows, pl.ds(kk * block_size, block_size)] = jnp.where(
                slot >= 0, block, jnp.zeros_like(block)
            )

    out_ref[...] += jnp.dot(stage_ref[...], panel_ref[...], preferred_element_type=jnp.float32)


def dense_rows(first, slot_of, gathered, panel, share, width=8, col_parts=1, col_part=0):
    slot_count = gathered.shape[0]
    block_size = gathered.shape[-1]
    out_cols = panel.shape[1] // col_parts
    return pl.pallas_call(
        dense_rows_kernel,
        out_shape=jax.ShapeDtypeStruct((share * block_size, out_cols), jnp.float32),
        grid_spec=pltpu.PrefetchScalarGridSpec(
            num_scalar_prefetch=2,
            grid=(panel.shape[0] // (width * block_size),),
            in_specs=[
                pl.BlockSpec((slot_count, share * block_size, block_size),
                             lambda j, f, t: (0, f[0] // share, 0), pipeline_mode=pl.Buffered(1)),
                pl.BlockSpec((width * block_size, out_cols), lambda j, f, t: (j, col_part)),
            ],
            out_specs=pl.BlockSpec((share * block_size, out_cols), lambda j, f, t: (0, 0)),
            scratch_shapes=[pltpu.VMEM((share * block_size, width * block_size), jnp.bfloat16)],
        ),
        compiler_params=pltpu.CompilerParams(vmem_limit_bytes=48 * 1024 * 1024),
        cost_estimate=pl.CostEstimate(
            flops=2 * share * block_size * panel.shape[0] * out_cols,
            transcendentals=0,
            bytes_accessed=slot_count * share * block_size * block_size * 2 + panel.size * 2 // col_parts + share * block_size * out_cols * 4,
        ),
    )(first, slot_of, gathered, panel)


COL_FACTORS = (8, 4, 2)
COL_PARTS = ("col_z", "col_y", "col_x")


def gather_slots(packed, split):
    if split:
        packed = lax.all_gather(packed, COL_PARTS[2], axis=0, tiled=True)
        return lax.all_gather(packed, COL_PARTS[:2], axis=0, tiled=True)
    return lax.all_gather(packed, "col", axis=0, tiled=True)


def body(flow_cols, flow_vals, window_flow, split):
    row = lax.axis_index("row")
    layer = lax.axis_index("layer")
    n_layer = lax.axis_size("layer")
    own_g = window_flow[0]
    half_rows = own_g.shape[0]
    other_g = lax.ppermute(own_g, "row", perm=[(0, 1), (1, 0)])
    panel = jnp.zeros((2 * half_rows, own_g.shape[1]), own_g.dtype)
    panel = lax.dynamic_update_slice_in_dim(panel, own_g, row * half_rows, 0)
    panel = lax.dynamic_update_slice_in_dim(panel, other_g, (1 - row) * half_rows, 0)

    block_size = flow_vals.shape[-1]
    block_count = panel.shape[0] // block_size
    row_blocks = flow_vals.shape[0]
    stacked = flow_vals.reshape(1, row_blocks * block_size, block_size)
    col_tile = jnp.zeros((1, 16, block_size), jnp.bfloat16)
    col_tile = col_tile.at[0, 0, :row_blocks].set(flow_cols.reshape(row_blocks).astype(jnp.bfloat16))
    packed = jnp.concatenate([stacked, col_tile], axis=1)
    gathered = gather_slots(packed, split)
    slot_cols = gathered[:, row_blocks * block_size, :row_blocks].astype(jnp.int32).T
    slot_count = gathered.shape[0]
    hit = slot_cols[:, :, None] == jnp.arange(block_count, dtype=jnp.int32)[None, None, :]
    slot_ids = jnp.arange(slot_count, dtype=jnp.int32)[None, :, None]
    slot_of = jnp.max(jnp.where(hit, slot_ids, -1), axis=1)

    share = row_blocks // n_layer
    send_first = ((1 - layer) * share).astype(jnp.int32).reshape(1)
    keep_first = (layer * share).astype(jnp.int32).reshape(1)

    def expand(first):
        return dense_rows(first, slot_of, gathered, panel, share)

    received = []
    for part in range(2):
        sent = dense_rows(send_first, slot_of, gathered, panel, share, col_parts=2, col_part=part)
        received.append(lax.ppermute(sent, "layer", perm=[(0, 1), (1, 0)]))
    summed = expand(keep_first) + jnp.concatenate(received, axis=1)
    squares = summed * summed
    total_rows = row_blocks * block_size * lax.axis_size("row")
    column_sums = lax.psum(jnp.sum(squares, axis=0), ("row", "layer"))
    return squares / (column_sums / total_rows + 1e-06)


def solution(mesh):
    split = mesh.shape["col"] == COL_FACTORS[0] * COL_FACTORS[1] * COL_FACTORS[2]
    if split:
        devices = mesh.devices.reshape(
            (mesh.shape["row"],) + COL_FACTORS + (mesh.shape["layer"],)
        )
        mesh = Mesh(devices, ("row",) + COL_PARTS + ("layer",))
        col = COL_PARTS
    else:
        col = "col"
    placed = (
        P("row", "layer", col),
        P("row", "layer", col, None, None),
        P("layer", "row", col),
    )
    return jax.shard_map(
        lambda c, v, w: body(c, v, w, split),
        mesh=mesh, in_specs=placed, out_specs=P(("row", "layer"), col), check_vma=False,
    )
```

```python
import jax
import jax.numpy as jnp
from jax.experimental import pallas as pl
from jax.experimental.pallas import tpu as pltpu
from jax import lax
from jax.sharding import Mesh, PartitionSpec as P


def dense_rows_kernel(first_ref, slot_of_ref, vals_hbm, panel_ref, out_ref, stage_ref, sems):
    share = stage_ref.shape[1] // vals_hbm.shape[-1]
    block_size = vals_hbm.shape[-1]
    width = stage_ref.shape[2] // block_size
    chunks = pl.num_programs(0)
    j = pl.program_id(0)
    buf = j % 2
    first = first_ref[0]

    def copy(chunk, slot_buf, i, kk, slot):
        return pltpu.make_async_copy(
            vals_hbm.at[slot, pl.ds((first + i) * block_size, block_size), :],
            stage_ref.at[slot_buf, pl.ds(i * block_size, block_size), pl.ds(kk * block_size, block_size)],
            sems.at[slot_buf, i, kk],
        )

    def fetch(chunk, slot_buf):
        for i in range(share):
            for kk in range(width):
                slot = slot_of_ref[first + i, chunk * width + kk]

                @pl.when(slot >= 0)
                def _():
                    copy(chunk, slot_buf, i, kk, slot).start()

    @pl.when(j == 0)
    def _():
        out_ref[...] = jnp.zeros_like(out_ref)
        fetch(0, 0)

    @pl.when(j + 1 < chunks)
    def _():
        fetch(j + 1, 1 - buf)

    for i in range(share):
        for kk in range(width):
            slot = slot_of_ref[first + i, j * width + kk]

            @pl.when(slot >= 0)
            def _():
                copy(j, buf, i, kk, slot).wait()

            @pl.when(slot < 0)
            def _():
                stage_ref[buf, pl.ds(i * block_size, block_size), pl.ds(kk * block_size, block_size)] = (
                    jnp.zeros((block_size, block_size), stage_ref.dtype)
                )

    out_ref[...] += jnp.dot(stage_ref[buf], panel_ref[...], preferred_element_type=jnp.float32)


def dense_rows(first, slot_of, gathered, panel, share, width=8, col_parts=1, col_part=0):
    block_size = gathered.shape[-1]
    out_cols = panel.shape[1] // col_parts
    depth = width * block_size
    return pl.pallas_call(
        dense_rows_kernel,
        out_shape=jax.ShapeDtypeStruct((share * block_size, out_cols), jnp.float32),
        grid_spec=pltpu.PrefetchScalarGridSpec(
            num_scalar_prefetch=2,
            grid=(panel.shape[0] // depth,),
            in_specs=[
                pl.BlockSpec(memory_space=pl.ANY),
                pl.BlockSpec((depth, out_cols), lambda j, f, t: (j, col_part)),
            ],
            out_specs=pl.BlockSpec((share * block_size, out_cols), lambda j, f, t: (0, 0)),
            scratch_shapes=[
                pltpu.VMEM((2, share * block_size, depth), jnp.bfloat16),
                pltpu.SemaphoreType.DMA((2, share, width)),
            ],
        ),
        compiler_params=pltpu.CompilerParams(vmem_limit_bytes=48 * 1024 * 1024),
        cost_estimate=pl.CostEstimate(
            flops=2 * share * block_size * panel.shape[0] * out_cols,
            transcendentals=0,
            bytes_accessed=share * block_size * panel.shape[0] * 2 + panel.size * 2 // col_parts + share * block_size * out_cols * 4,
        ),
    )(first, slot_of, gathered, panel)


COL_FACTORS = (8, 4, 2)
COL_PARTS = ("col_z", "col_y", "col_x")


def gather_slots(packed, split):
    if split:
        packed = lax.all_gather(packed, COL_PARTS[2], axis=0, tiled=True)
        return lax.all_gather(packed, COL_PARTS[:2], axis=0, tiled=True)
    return lax.all_gather(packed, "col", axis=0, tiled=True)


def body(flow_cols, flow_vals, window_flow, split):
    row = lax.axis_index("row")
    layer = lax.axis_index("layer")
    n_layer = lax.axis_size("layer")
    own_g = window_flow[0]
    half_rows = own_g.shape[0]
    other_g = lax.ppermute(own_g, "row", perm=[(0, 1), (1, 0)])
    panel = jnp.zeros((2 * half_rows, own_g.shape[1]), own_g.dtype)
    panel = lax.dynamic_update_slice_in_dim(panel, own_g, row * half_rows, 0)
    panel = lax.dynamic_update_slice_in_dim(panel, other_g, (1 - row) * half_rows, 0)

    block_size = flow_vals.shape[-1]
    block_count = panel.shape[0] // block_size
    row_blocks = flow_vals.shape[0]
    stacked = flow_vals.reshape(1, row_blocks * block_size, block_size)
    col_tile = jnp.zeros((1, 16, block_size), jnp.bfloat16)
    col_tile = col_tile.at[0, 0, :row_blocks].set(flow_cols.reshape(row_blocks).astype(jnp.bfloat16))
    packed = jnp.concatenate([stacked, col_tile], axis=1)
    gathered = gather_slots(packed, split)
    slot_cols = gathered[:, row_blocks * block_size, :row_blocks].astype(jnp.int32).T
    slot_count = gathered.shape[0]
    hit = slot_cols[:, :, None] == jnp.arange(block_count, dtype=jnp.int32)[None, None, :]
    slot_ids = jnp.arange(slot_count, dtype=jnp.int32)[None, :, None]
    slot_of = jnp.max(jnp.where(hit, slot_ids, -1), axis=1)

    share = row_blocks // n_layer
    send_first = ((1 - layer) * share).astype(jnp.int32).reshape(1)
    keep_first = (layer * share).astype(jnp.int32).reshape(1)

    def expand(first):
        return dense_rows(first, slot_of, gathered, panel, share)

    received = []
    for part in range(2):
        sent = dense_rows(send_first, slot_of, gathered, panel, share, col_parts=2, col_part=part)
        received.append(lax.ppermute(sent, "layer", perm=[(0, 1), (1, 0)]))
    summed = expand(keep_first) + jnp.concatenate(received, axis=1)
    squares = summed * summed
    total_rows = row_blocks * block_size * lax.axis_size("row")
    column_sums = lax.psum(jnp.sum(squares, axis=0), ("row", "layer"))
    return squares / (column_sums / total_rows + 1e-06)


def solution(mesh):
    split = mesh.shape["col"] == COL_FACTORS[0] * COL_FACTORS[1] * COL_FACTORS[2]
    if split:
        devices = mesh.devices.reshape(
            (mesh.shape["row"],) + COL_FACTORS + (mesh.shape["layer"],)
        )
        mesh = Mesh(devices, ("row",) + COL_PARTS + ("layer",))
        col = COL_PARTS
    else:
        col = "col"
    placed = (
        P("row", "layer", col),
        P("row", "layer", col, None, None),
        P("layer", "row", col),
    )
    return jax.shard_map(
        lambda c, v, w: body(c, v, w, split),
        mesh=mesh, in_specs=placed, out_specs=P(("row", "layer"), col), check_vma=False,
    )
```

```python
import jax
import jax.numpy as jnp
from jax.experimental import pallas as pl
from jax.experimental.pallas import tpu as pltpu
from jax import lax
from jax.sharding import Mesh, PartitionSpec as P


def dense_rows_kernel(first_ref, slot_of_ref, vals_ref, panel_ref, out_ref, stage_ref):
    block_size = vals_ref.shape[-1]
    share = vals_ref.shape[1] // block_size
    width = stage_ref.shape[1] // block_size
    j = pl.program_id(0)
    first = first_ref[0]

    @pl.when(j == 0)
    def _():
        out_ref[...] = jnp.zeros_like(out_ref)

    for i in range(share):
        for kk in range(width):
            slot = slot_of_ref[first + i, j * width + kk]
            rows = pl.ds(i * block_size, block_size)
            block = vals_ref[jnp.maximum(slot, 0), rows, :]
            stage_ref[rows, pl.ds(kk * block_size, block_size)] = jnp.where(
                slot >= 0, block, jnp.zeros_like(block)
            )

    out_ref[...] += jnp.dot(stage_ref[...], panel_ref[...], preferred_element_type=jnp.float32)


def dense_rows(first, slot_of, gathered, panel, share, width=16, col_parts=1, col_part=0):
    slot_count = gathered.shape[0]
    block_size = gathered.shape[-1]
    out_cols = panel.shape[1] // col_parts
    return pl.pallas_call(
        dense_rows_kernel,
        out_shape=jax.ShapeDtypeStruct((share * block_size, out_cols), jnp.float32),
        grid_spec=pltpu.PrefetchScalarGridSpec(
            num_scalar_prefetch=2,
            grid=(panel.shape[0] // (width * block_size),),
            in_specs=[
                pl.BlockSpec((slot_count, share * block_size, block_size),
                             lambda j, f, t: (0, f[0] // share, 0), pipeline_mode=pl.Buffered(1)),
                pl.BlockSpec((width * block_size, out_cols), lambda j, f, t: (j, col_part)),
            ],
            out_specs=pl.BlockSpec((share * block_size, out_cols), lambda j, f, t: (0, 0)),
            scratch_shapes=[pltpu.VMEM((share * block_size, width * block_size), jnp.bfloat16)],
        ),
        compiler_params=pltpu.CompilerParams(vmem_limit_bytes=48 * 1024 * 1024),
        cost_estimate=pl.CostEstimate(
            flops=2 * share * block_size * panel.shape[0] * out_cols,
            transcendentals=0,
            bytes_accessed=slot_count * share * block_size * block_size * 2 + panel.size * 2 // col_parts + share * block_size * out_cols * 4,
        ),
    )(first, slot_of, gathered, panel)


COL_FACTORS = (8, 4, 2)
COL_PARTS = ("col_z", "col_y", "col_x")


def gather_slots(packed, split):
    if split:
        packed = lax.all_gather(packed, COL_PARTS[2], axis=0, tiled=True)
        return lax.all_gather(packed, COL_PARTS[:2], axis=0, tiled=True)
    return lax.all_gather(packed, "col", axis=0, tiled=True)


def body(flow_cols, flow_vals, window_flow, split):
    row = lax.axis_index("row")
    layer = lax.axis_index("layer")
    n_layer = lax.axis_size("layer")
    own_g = window_flow[0]
    half_rows = own_g.shape[0]
    other_g = lax.ppermute(own_g, "row", perm=[(0, 1), (1, 0)])
    panel = jnp.zeros((2 * half_rows, own_g.shape[1]), own_g.dtype)
    panel = lax.dynamic_update_slice_in_dim(panel, own_g, row * half_rows, 0)
    panel = lax.dynamic_update_slice_in_dim(panel, other_g, (1 - row) * half_rows, 0)

    block_size = flow_vals.shape[-1]
    block_count = panel.shape[0] // block_size
    row_blocks = flow_vals.shape[0]
    stacked = flow_vals.reshape(1, row_blocks * block_size, block_size)
    col_tile = jnp.zeros((1, 16, block_size), jnp.bfloat16)
    col_tile = col_tile.at[0, 0, :row_blocks].set(flow_cols.reshape(row_blocks).astype(jnp.bfloat16))
    packed = jnp.concatenate([stacked, col_tile], axis=1)
    gathered = gather_slots(packed, split)
    slot_cols = gathered[:, row_blocks * block_size, :row_blocks].astype(jnp.int32).T
    slot_count = gathered.shape[0]
    hit = slot_cols[:, :, None] == jnp.arange(block_count, dtype=jnp.int32)[None, None, :]
    slot_ids = jnp.arange(slot_count, dtype=jnp.int32)[None, :, None]
    slot_of = jnp.max(jnp.where(hit, slot_ids, -1), axis=1)

    share = row_blocks // n_layer
    send_first = ((1 - layer) * share).astype(jnp.int32).reshape(1)
    keep_first = (layer * share).astype(jnp.int32).reshape(1)

    def expand(first):
        return dense_rows(first, slot_of, gathered, panel, share)

    received = []
    for part in range(2):
        sent = dense_rows(send_first, slot_of, gathered, panel, share, col_parts=2, col_part=part)
        received.append(lax.ppermute(sent, "layer", perm=[(0, 1), (1, 0)]))
    summed = expand(keep_first) + jnp.concatenate(received, axis=1)
    squares = summed * summed
    total_rows = row_blocks * block_size * lax.axis_size("row")
    column_sums = lax.psum(jnp.sum(squares, axis=0), ("row", "layer"))
    return squares / (column_sums / total_rows + 1e-06)


def solution(mesh):
    split = mesh.shape["col"] == COL_FACTORS[0] * COL_FACTORS[1] * COL_FACTORS[2]
    if split:
        devices = mesh.devices.reshape(
            (mesh.shape["row"],) + COL_FACTORS + (mesh.shape["layer"],)
        )
        mesh = Mesh(devices, ("row",) + COL_PARTS + ("layer",))
        col = COL_PARTS
    else:
        col = "col"
    placed = (
        P("row", "layer", col),
        P("row", "layer", col, None, None),
        P("layer", "row", col),
    )
    return jax.shard_map(
        lambda c, v, w: body(c, v, w, split),
        mesh=mesh, in_specs=placed, out_specs=P(("row", "layer"), col), check_vma=False,
    )
```

```python
import jax
import jax.numpy as jnp
from jax.experimental import pallas as pl
from jax.experimental.pallas import tpu as pltpu
from jax import lax
from jax.sharding import Mesh, PartitionSpec as P


def dense_rows_kernel(first_ref, slot_of_ref, vals_ref, panel_ref, out_ref, stage_ref):
    block_size = vals_ref.shape[-1]
    share = vals_ref.shape[1] // block_size
    width = stage_ref.shape[1] // block_size
    j = pl.program_id(0)
    first = first_ref[0]

    @pl.when(j == 0)
    def _():
        out_ref[...] = jnp.zeros_like(out_ref)

    for i in range(share):
        for kk in range(width):
            slot = slot_of_ref[first + i, j * width + kk]
            rows = pl.ds(i * block_size, block_size)
            block = vals_ref[jnp.maximum(slot, 0), rows, :]
            stage_ref[rows, pl.ds(kk * block_size, block_size)] = jnp.where(
                slot >= 0, block, jnp.zeros_like(block)
            )

    out_ref[...] += jnp.dot(stage_ref[...], panel_ref[...], preferred_element_type=jnp.float32)


def dense_rows(first, slot_of, gathered, panel, share, width=32, col_parts=1, col_part=0):
    slot_count = gathered.shape[0]
    block_size = gathered.shape[-1]
    out_cols = panel.shape[1] // col_parts
    return pl.pallas_call(
        dense_rows_kernel,
        out_shape=jax.ShapeDtypeStruct((share * block_size, out_cols), jnp.float32),
        grid_spec=pltpu.PrefetchScalarGridSpec(
            num_scalar_prefetch=2,
            grid=(panel.shape[0] // (width * block_size),),
            in_specs=[
                pl.BlockSpec((slot_count, share * block_size, block_size),
                             lambda j, f, t: (0, f[0] // share, 0), pipeline_mode=pl.Buffered(1)),
                pl.BlockSpec((width * block_size, out_cols), lambda j, f, t: (j, col_part)),
            ],
            out_specs=pl.BlockSpec((share * block_size, out_cols), lambda j, f, t: (0, 0)),
            scratch_shapes=[pltpu.VMEM((share * block_size, width * block_size), jnp.bfloat16)],
        ),
        compiler_params=pltpu.CompilerParams(vmem_limit_bytes=48 * 1024 * 1024),
        cost_estimate=pl.CostEstimate(
            flops=2 * share * block_size * panel.shape[0] * out_cols,
            transcendentals=0,
            bytes_accessed=slot_count * share * block_size * block_size * 2 + panel.size * 2 // col_parts + share * block_size * out_cols * 4,
        ),
    )(first, slot_of, gathered, panel)


COL_FACTORS = (8, 4, 2)
COL_PARTS = ("col_z", "col_y", "col_x")


def gather_slots(packed, split):
    if split:
        packed = lax.all_gather(packed, COL_PARTS[2], axis=0, tiled=True)
        return lax.all_gather(packed, COL_PARTS[:2], axis=0, tiled=True)
    return lax.all_gather(packed, "col", axis=0, tiled=True)


def body(flow_cols, flow_vals, window_flow, split):
    row = lax.axis_index("row")
    layer = lax.axis_index("layer")
    n_layer = lax.axis_size("layer")
    own_g = window_flow[0]
    half_rows = own_g.shape[0]
    other_g = lax.ppermute(own_g, "row", perm=[(0, 1), (1, 0)])
    panel = jnp.zeros((2 * half_rows, own_g.shape[1]), own_g.dtype)
    panel = lax.dynamic_update_slice_in_dim(panel, own_g, row * half_rows, 0)
    panel = lax.dynamic_update_slice_in_dim(panel, other_g, (1 - row) * half_rows, 0)

    block_size = flow_vals.shape[-1]
    block_count = panel.shape[0] // block_size
    row_blocks = flow_vals.shape[0]
    stacked = flow_vals.reshape(1, row_blocks * block_size, block_size)
    col_tile = jnp.zeros((1, 16, block_size), jnp.bfloat16)
    col_tile = col_tile.at[0, 0, :row_blocks].set(flow_cols.reshape(row_blocks).astype(jnp.bfloat16))
    packed = jnp.concatenate([stacked, col_tile], axis=1)
    gathered = gather_slots(packed, split)
    slot_cols = gathered[:, row_blocks * block_size, :row_blocks].astype(jnp.int32).T
    slot_count = gathered.shape[0]
    hit = slot_cols[:, :, None] == jnp.arange(block_count, dtype=jnp.int32)[None, None, :]
    slot_ids = jnp.arange(slot_count, dtype=jnp.int32)[None, :, None]
    slot_of = jnp.max(jnp.where(hit, slot_ids, -1), axis=1)

    share = row_blocks // n_layer
    send_first = ((1 - layer) * share).astype(jnp.int32).reshape(1)
    keep_first = (layer * share).astype(jnp.int32).reshape(1)

    def expand(first):
        return dense_rows(first, slot_of, gathered, panel, share)

    received = []
    for part in range(2):
        sent = dense_rows(send_first, slot_of, gathered, panel, share, col_parts=2, col_part=part)
        received.append(lax.ppermute(sent, "layer", perm=[(0, 1), (1, 0)]))
    summed = expand(keep_first) + jnp.concatenate(received, axis=1)
    squares = summed * summed
    total_rows = row_blocks * block_size * lax.axis_size("row")
    column_sums = lax.psum(jnp.sum(squares, axis=0), ("row", "layer"))
    return squares / (column_sums / total_rows + 1e-06)


def solution(mesh):
    split = mesh.shape["col"] == COL_FACTORS[0] * COL_FACTORS[1] * COL_FACTORS[2]
    if split:
        devices = mesh.devices.reshape(
            (mesh.shape["row"],) + COL_FACTORS + (mesh.shape["layer"],)
        )
        mesh = Mesh(devices, ("row",) + COL_PARTS + ("layer",))
        col = COL_PARTS
    else:
        col = "col"
    placed = (
        P("row", "layer", col),
        P("row", "layer", col, None, None),
        P("layer", "row", col),
    )
    return jax.shard_map(
        lambda c, v, w: body(c, v, w, split),
        mesh=mesh, in_specs=placed, out_specs=P(("row", "layer"), col), check_vma=False,
    )
```

```python
import jax
import jax.numpy as jnp
from jax.experimental import pallas as pl
from jax.experimental.pallas import tpu as pltpu
from jax import lax
from jax.sharding import Mesh, PartitionSpec as P


def dense_rows_kernel(first_ref, slot_of_ref, vals_ref, panel_ref, out_ref, stage_ref):
    block_size = vals_ref.shape[-1]
    share = vals_ref.shape[1] // block_size
    width = stage_ref.shape[1] // block_size
    j = pl.program_id(0)
    first = first_ref[0]

    @pl.when(j == 0)
    def _():
        out_ref[...] = jnp.zeros_like(out_ref)

    for i in range(share):
        for kk in range(width):
            slot = slot_of_ref[first + i, j * width + kk]
            rows = pl.ds(i * block_size, block_size)
            block = vals_ref[jnp.maximum(slot, 0), rows, :]
            stage_ref[rows, pl.ds(kk * block_size, block_size)] = jnp.where(
                slot >= 0, block, jnp.zeros_like(block)
            )

    out_ref[...] += jnp.dot(stage_ref[...], panel_ref[...], preferred_element_type=jnp.float32)


def dense_rows(first, slot_of, gathered, panel, share, width=32, col_parts=1, col_part=0):
    slot_count = gathered.shape[0]
    block_size = gathered.shape[-1]
    out_cols = panel.shape[1] // col_parts
    return pl.pallas_call(
        dense_rows_kernel,
        out_shape=jax.ShapeDtypeStruct((share * block_size, out_cols), jnp.float32),
        grid_spec=pltpu.PrefetchScalarGridSpec(
            num_scalar_prefetch=2,
            grid=(panel.shape[0] // (width * block_size),),
            in_specs=[
                pl.BlockSpec((slot_count, share * block_size, block_size),
                             lambda j, f, t: (0, f[0] // share, 0), pipeline_mode=pl.Buffered(1)),
                pl.BlockSpec((width * block_size, out_cols), lambda j, f, t: (j, col_part)),
            ],
            out_specs=pl.BlockSpec((share * block_size, out_cols), lambda j, f, t: (0, 0)),
            scratch_shapes=[pltpu.VMEM((share * block_size, width * block_size), jnp.bfloat16)],
        ),
        compiler_params=pltpu.CompilerParams(vmem_limit_bytes=48 * 1024 * 1024),
        cost_estimate=pl.CostEstimate(
            flops=2 * share * block_size * panel.shape[0] * out_cols,
            transcendentals=0,
            bytes_accessed=slot_count * share * block_size * block_size * 2 + panel.size * 2 // col_parts + share * block_size * out_cols * 4,
        ),
    )(first, slot_of, gathered, panel)


COL_FACTORS = (8, 4, 2)
COL_PARTS = ("col_z", "col_y", "col_x")


def gather_slots(packed, split):
    if split:
        packed = lax.all_gather(packed, COL_PARTS[2], axis=0, tiled=True)
        return lax.all_gather(packed, COL_PARTS[:2], axis=0, tiled=True)
    return lax.all_gather(packed, "col", axis=0, tiled=True)


def body(flow_cols, flow_vals, window_flow, split):
    row = lax.axis_index("row")
    layer = lax.axis_index("layer")
    n_layer = lax.axis_size("layer")
    own_g = window_flow[0]
    half_rows = own_g.shape[0]
    other_g = lax.ppermute(own_g, "row", perm=[(0, 1), (1, 0)])
    panel = jnp.zeros((2 * half_rows, own_g.shape[1]), own_g.dtype)
    panel = lax.dynamic_update_slice_in_dim(panel, own_g, row * half_rows, 0)
    panel = lax.dynamic_update_slice_in_dim(panel, other_g, (1 - row) * half_rows, 0)

    block_size = flow_vals.shape[-1]
    block_count = panel.shape[0] // block_size
    row_blocks = flow_vals.shape[0]
    stacked = flow_vals.reshape(1, row_blocks * block_size, block_size)
    col_tile = jnp.zeros((1, 16, block_size), jnp.bfloat16)
    col_tile = col_tile.at[0, 0, :row_blocks].set(flow_cols.reshape(row_blocks).astype(jnp.bfloat16))
    packed = jnp.concatenate([stacked, col_tile], axis=1)
    gathered = gather_slots(packed, split)
    slot_cols = gathered[:, row_blocks * block_size, :row_blocks].astype(jnp.int32).T
    slot_count = gathered.shape[0]
    hit = slot_cols[:, :, None] == jnp.arange(block_count, dtype=jnp.int32)[None, None, :]
    slot_ids = jnp.arange(slot_count, dtype=jnp.int32)[None, :, None]
    slot_of = jnp.max(jnp.where(hit, slot_ids, -1), axis=1)

    share = row_blocks // n_layer
    send_first = ((1 - layer) * share).astype(jnp.int32).reshape(1)
    keep_first = (layer * share).astype(jnp.int32).reshape(1)

    def expand(first):
        return dense_rows(first, slot_of, gathered, panel, share)

    received = []
    for part in range(2):
        sent = dense_rows(send_first, slot_of, gathered, panel, share, col_parts=2, col_part=part)
        received.append(lax.ppermute(sent, "layer", perm=[(0, 1), (1, 0)]))
    summed = expand(keep_first) + jnp.concatenate(received, axis=1)
    squares = summed * summed
    total_rows = row_blocks * block_size * lax.axis_size("row")
    column_sums = lax.psum(lax.psum(jnp.sum(squares, axis=0), "row"), "layer")
    return squares / (column_sums / total_rows + 1e-06)


def solution(mesh):
    split = mesh.shape["col"] == COL_FACTORS[0] * COL_FACTORS[1] * COL_FACTORS[2]
    if split:
        devices = mesh.devices.reshape(
            (mesh.shape["row"],) + COL_FACTORS + (mesh.shape["layer"],)
        )
        mesh = Mesh(devices, ("row",) + COL_PARTS + ("layer",))
        col = COL_PARTS
    else:
        col = "col"
    placed = (
        P("row", "layer", col),
        P("row", "layer", col, None, None),
        P("layer", "row", col),
    )
    return jax.shard_map(
        lambda c, v, w: body(c, v, w, split),
        mesh=mesh, in_specs=placed, out_specs=P(("row", "layer"), col), check_vma=False,
    )
```

```python
import jax
import jax.numpy as jnp
from jax.experimental import pallas as pl
from jax.experimental.pallas import tpu as pltpu
from jax import lax
from jax.sharding import Mesh, PartitionSpec as P


def dense_rows_kernel(first_ref, slot_of_ref, vals_ref, panel_ref, out_ref, stage_ref):
    block_size = vals_ref.shape[-1]
    share = vals_ref.shape[1] // block_size
    width = stage_ref.shape[1] // block_size
    j = pl.program_id(0)
    first = first_ref[0]

    @pl.when(j == 0)
    def _():
        out_ref[...] = jnp.zeros_like(out_ref)

    for i in range(share):
        for kk in range(width):
            slot = slot_of_ref[first + i, j * width + kk]
            rows = pl.ds(i * block_size, block_size)
            block = vals_ref[jnp.maximum(slot, 0), rows, :]
            stage_ref[rows, pl.ds(kk * block_size, block_size)] = jnp.where(
                slot >= 0, block, jnp.zeros_like(block)
            )

    out_ref[...] += jnp.dot(stage_ref[...], panel_ref[...], preferred_element_type=jnp.float32)


def dense_rows(first, slot_of, gathered, panel, share, width=32, col_parts=1, col_part=0):
    slot_count = gathered.shape[0]
    block_size = gathered.shape[-1]
    out_cols = panel.shape[1] // col_parts
    return pl.pallas_call(
        dense_rows_kernel,
        out_shape=jax.ShapeDtypeStruct((share * block_size, out_cols), jnp.float32),
        grid_spec=pltpu.PrefetchScalarGridSpec(
            num_scalar_prefetch=2,
            grid=(panel.shape[0] // (width * block_size),),
            in_specs=[
                pl.BlockSpec((slot_count, share * block_size, block_size),
                             lambda j, f, t: (0, f[0] // share, 0), pipeline_mode=pl.Buffered(1)),
                pl.BlockSpec((width * block_size, out_cols), lambda j, f, t: (j, col_part)),
            ],
            out_specs=pl.BlockSpec((share * block_size, out_cols), lambda j, f, t: (0, 0)),
            scratch_shapes=[pltpu.VMEM((share * block_size, width * block_size), jnp.bfloat16)],
        ),
        compiler_params=pltpu.CompilerParams(vmem_limit_bytes=48 * 1024 * 1024),
        cost_estimate=pl.CostEstimate(
            flops=2 * share * block_size * panel.shape[0] * out_cols,
            transcendentals=0,
            bytes_accessed=slot_count * share * block_size * block_size * 2 + panel.size * 2 // col_parts + share * block_size * out_cols * 4,
        ),
    )(first, slot_of, gathered, panel)


COL_FACTORS = (8, 4, 2)
COL_PARTS = ("col_z", "col_y", "col_x")


def gather_slots(packed, split):
    if split:
        packed = lax.all_gather(packed, COL_PARTS[2], axis=0, tiled=True)
        return lax.all_gather(packed, COL_PARTS[:2], axis=0, tiled=True)
    return lax.all_gather(packed, "col", axis=0, tiled=True)


def body(flow_cols, flow_vals, window_flow, split):
    row = lax.axis_index("row")
    layer = lax.axis_index("layer")
    n_layer = lax.axis_size("layer")
    own_g = window_flow[0]
    half_rows = own_g.shape[0]
    other_g = lax.ppermute(own_g, "row", perm=[(0, 1), (1, 0)])
    panel = jnp.zeros((2 * half_rows, own_g.shape[1]), own_g.dtype)
    panel = lax.dynamic_update_slice_in_dim(panel, own_g, row * half_rows, 0)
    panel = lax.dynamic_update_slice_in_dim(panel, other_g, (1 - row) * half_rows, 0)

    block_size = flow_vals.shape[-1]
    block_count = panel.shape[0] // block_size
    row_blocks = flow_vals.shape[0]
    stacked = flow_vals.reshape(1, row_blocks * block_size, block_size)
    col_tile = jnp.zeros((1, 16, block_size), jnp.bfloat16)
    col_tile = col_tile.at[0, 0, :row_blocks].set(flow_cols.reshape(row_blocks).astype(jnp.bfloat16))
    packed = jnp.concatenate([stacked, col_tile], axis=1)
    gathered = gather_slots(packed, split)
    slot_cols = gathered[:, row_blocks * block_size, :row_blocks].astype(jnp.int32).T
    slot_count = gathered.shape[0]
    hit = slot_cols[:, :, None] == jnp.arange(block_count, dtype=jnp.int32)[None, None, :]
    slot_ids = jnp.arange(slot_count, dtype=jnp.int32)[None, :, None]
    slot_of = jnp.max(jnp.where(hit, slot_ids, -1), axis=1)

    share = row_blocks // n_layer
    send_first = ((1 - layer) * share).astype(jnp.int32).reshape(1)
    keep_first = (layer * share).astype(jnp.int32).reshape(1)

    def expand(first):
        return dense_rows(first, slot_of, gathered, panel, share)

    received = []
    for parts, part in ((4, 0), (4, 1), (2, 1)):
        sent = dense_rows(send_first, slot_of, gathered, panel, share, col_parts=parts, col_part=part)
        received.append(lax.ppermute(sent, "layer", perm=[(0, 1), (1, 0)]))
    summed = expand(keep_first) + jnp.concatenate(received, axis=1)
    squares = summed * summed
    total_rows = row_blocks * block_size * lax.axis_size("row")
    column_sums = lax.psum(lax.psum(jnp.sum(squares, axis=0), "row"), "layer")
    return squares / (column_sums / total_rows + 1e-06)


def solution(mesh):
    split = mesh.shape["col"] == COL_FACTORS[0] * COL_FACTORS[1] * COL_FACTORS[2]
    if split:
        devices = mesh.devices.reshape(
            (mesh.shape["row"],) + COL_FACTORS + (mesh.shape["layer"],)
        )
        mesh = Mesh(devices, ("row",) + COL_PARTS + ("layer",))
        col = COL_PARTS
    else:
        col = "col"
    placed = (
        P("row", "layer", col),
        P("row", "layer", col, None, None),
        P("layer", "row", col),
    )
    return jax.shard_map(
        lambda c, v, w: body(c, v, w, split),
        mesh=mesh, in_specs=placed, out_specs=P(("row", "layer"), col), check_vma=False,
    )
```

```python
import jax
import jax.numpy as jnp
from jax.experimental import pallas as pl
from jax.experimental.pallas import tpu as pltpu
from jax import lax
from jax.sharding import Mesh, PartitionSpec as P


def dense_rows_kernel(first_ref, slot_of_ref, vals_ref, panel_ref, out_ref, stage_ref):
    block_size = vals_ref.shape[-1]
    share = vals_ref.shape[1] // block_size
    width = stage_ref.shape[1] // block_size
    j = pl.program_id(0)
    first = first_ref[0]

    @pl.when(j == 0)
    def _():
        out_ref[...] = jnp.zeros_like(out_ref)

    for i in range(share):
        for kk in range(width):
            slot = slot_of_ref[first + i, j * width + kk]
            rows = pl.ds(i * block_size, block_size)
            block = vals_ref[jnp.maximum(slot, 0), rows, :]
            stage_ref[rows, pl.ds(kk * block_size, block_size)] = jnp.where(
                slot >= 0, block, jnp.zeros_like(block)
            )

    out_ref[...] += jnp.dot(stage_ref[...], panel_ref[...], preferred_element_type=jnp.float32)


def dense_rows(first, slot_of, gathered, panel, share, width=32, col_parts=1, col_part=0):
    slot_count = gathered.shape[0]
    block_size = gathered.shape[-1]
    out_cols = panel.shape[1] // col_parts
    return pl.pallas_call(
        dense_rows_kernel,
        out_shape=jax.ShapeDtypeStruct((share * block_size, out_cols), jnp.float32),
        grid_spec=pltpu.PrefetchScalarGridSpec(
            num_scalar_prefetch=2,
            grid=(panel.shape[0] // (width * block_size),),
            in_specs=[
                pl.BlockSpec((slot_count, share * block_size, block_size),
                             lambda j, f, t: (0, f[0] // share, 0), pipeline_mode=pl.Buffered(1)),
                pl.BlockSpec((width * block_size, out_cols), lambda j, f, t: (j, col_part)),
            ],
            out_specs=pl.BlockSpec((share * block_size, out_cols), lambda j, f, t: (0, 0)),
            scratch_shapes=[pltpu.VMEM((share * block_size, width * block_size), jnp.bfloat16)],
        ),
        compiler_params=pltpu.CompilerParams(vmem_limit_bytes=48 * 1024 * 1024),
        cost_estimate=pl.CostEstimate(
            flops=2 * share * block_size * panel.shape[0] * out_cols,
            transcendentals=0,
            bytes_accessed=slot_count * share * block_size * block_size * 2 + panel.size * 2 // col_parts + share * block_size * out_cols * 4,
        ),
    )(first, slot_of, gathered, panel)


COL_FACTORS = (8, 4, 2)
COL_PARTS = ("col_z", "col_y", "col_x")


def gather_slots(packed, split):
    if split:
        packed = lax.all_gather(packed, COL_PARTS[2], axis=0, tiled=True)
        return lax.all_gather(packed, COL_PARTS[:2], axis=0, tiled=True)
    return lax.all_gather(packed, "col", axis=0, tiled=True)


def body(flow_cols, flow_vals, window_flow, split):
    row = lax.axis_index("row")
    layer = lax.axis_index("layer")
    n_layer = lax.axis_size("layer")
    own_g = window_flow[0]
    half_rows = own_g.shape[0]
    other_g = lax.ppermute(own_g, "row", perm=[(0, 1), (1, 0)])
    panel = jnp.zeros((2 * half_rows, own_g.shape[1]), own_g.dtype)
    panel = lax.dynamic_update_slice_in_dim(panel, own_g, row * half_rows, 0)
    panel = lax.dynamic_update_slice_in_dim(panel, other_g, (1 - row) * half_rows, 0)

    block_size = flow_vals.shape[-1]
    block_count = panel.shape[0] // block_size
    row_blocks = flow_vals.shape[0]
    stacked = flow_vals.reshape(1, row_blocks * block_size, block_size)
    col_tile = jnp.zeros((1, 16, block_size), jnp.bfloat16)
    col_tile = col_tile.at[0, 0, :row_blocks].set(flow_cols.reshape(row_blocks).astype(jnp.bfloat16))
    packed = jnp.concatenate([stacked, col_tile], axis=1)
    gathered = gather_slots(packed, split)
    slot_cols = gathered[:, row_blocks * block_size, :row_blocks].astype(jnp.int32).T
    slot_count = gathered.shape[0]
    hit = slot_cols[:, :, None] == jnp.arange(block_count, dtype=jnp.int32)[None, None, :]
    slot_ids = jnp.arange(slot_count, dtype=jnp.int32)[None, :, None]
    slot_of = jnp.max(jnp.where(hit, slot_ids, -1), axis=1)

    share = row_blocks // n_layer
    send_first = ((1 - layer) * share).astype(jnp.int32).reshape(1)
    keep_first = (layer * share).astype(jnp.int32).reshape(1)

    def expand(first):
        return dense_rows(first, slot_of, gathered, panel, share)

    received = []
    for part in range(2):
        sent = dense_rows(send_first, slot_of, gathered, panel, share, col_parts=2, col_part=part)
        received.append(lax.ppermute(sent, "layer", perm=[(0, 1), (1, 0)]))
    summed = expand(keep_first) + jnp.concatenate(received, axis=1)
    squares = summed * summed
    total_rows = row_blocks * block_size * lax.axis_size("row")
    column_sums = jnp.sum(squares, axis=0)
    for axis in ("row", "layer"):
        column_sums = column_sums + lax.ppermute(column_sums, axis, perm=[(0, 1), (1, 0)])
    return squares / (column_sums / total_rows + 1e-06)


def solution(mesh):
    split = mesh.shape["col"] == COL_FACTORS[0] * COL_FACTORS[1] * COL_FACTORS[2]
    if split:
        devices = mesh.devices.reshape(
            (mesh.shape["row"],) + COL_FACTORS + (mesh.shape["layer"],)
        )
        mesh = Mesh(devices, ("row",) + COL_PARTS + ("layer",))
        col = COL_PARTS
    else:
        col = "col"
    placed = (
        P("row", "layer", col),
        P("row", "layer", col, None, None),
        P("layer", "row", col),
    )
    return jax.shard_map(
        lambda c, v, w: body(c, v, w, split),
        mesh=mesh, in_specs=placed, out_specs=P(("row", "layer"), col), check_vma=False,
    )
```

```python
import jax
import jax.numpy as jnp
from jax.experimental import pallas as pl
from jax.experimental.pallas import tpu as pltpu
from jax import lax
from jax.sharding import Mesh, PartitionSpec as P


def dense_rows_kernel(first_ref, slot_of_ref, vals_ref, panel_ref, out_ref, stage_ref):
    block_size = vals_ref.shape[-1]
    group = vals_ref.shape[1] // block_size
    width = stage_ref.shape[1] // block_size
    p = pl.program_id(0)
    j = pl.program_id(1)
    first = first_ref[0] + p * group

    @pl.when(j == 0)
    def _():
        out_ref[...] = jnp.zeros_like(out_ref)

    for i in range(group):
        for kk in range(width):
            slot = slot_of_ref[first + i, j * width + kk]
            rows = pl.ds(i * block_size, block_size)
            block = vals_ref[jnp.maximum(slot, 0), rows, :]
            stage_ref[rows, pl.ds(kk * block_size, block_size)] = jnp.where(
                slot >= 0, block, jnp.zeros_like(block)
            )

    out_ref[...] += jnp.dot(stage_ref[...], panel_ref[...], preferred_element_type=jnp.float32)


def dense_rows(first, slot_of, gathered, panel, share, width=32, col_parts=1, col_part=0, group=None):
    group = share if group is None else group
    slot_count = gathered.shape[0]
    block_size = gathered.shape[-1]
    out_cols = panel.shape[1] // col_parts
    vals_mode = {"pipeline_mode": pl.Buffered(1)} if group == share else {}
    return pl.pallas_call(
        dense_rows_kernel,
        out_shape=jax.ShapeDtypeStruct((share * block_size, out_cols), jnp.float32),
        grid_spec=pltpu.PrefetchScalarGridSpec(
            num_scalar_prefetch=2,
            grid=(share // group, panel.shape[0] // (width * block_size)),
            in_specs=[
                pl.BlockSpec((slot_count, group * block_size, block_size),
                             lambda p, j, f, t: (0, f[0] // group + p, 0), **vals_mode),
                pl.BlockSpec((width * block_size, out_cols), lambda p, j, f, t: (j, col_part)),
            ],
            out_specs=pl.BlockSpec((group * block_size, out_cols), lambda p, j, f, t: (p, 0)),
            scratch_shapes=[pltpu.VMEM((group * block_size, width * block_size), jnp.bfloat16)],
        ),
        compiler_params=pltpu.CompilerParams(vmem_limit_bytes=48 * 1024 * 1024),
        cost_estimate=pl.CostEstimate(
            flops=2 * share * block_size * panel.shape[0] * out_cols,
            transcendentals=0,
            bytes_accessed=slot_count * share * block_size * block_size * 2
            + panel.size * 2 // col_parts * (share // group) + share * block_size * out_cols * 4,
        ),
    )(first, slot_of, gathered, panel)


COL_FACTORS = (8, 4, 2)
COL_PARTS = ("col_z", "col_y", "col_x")


def gather_slots(packed, split):
    if split:
        packed = lax.all_gather(packed, COL_PARTS[2], axis=0, tiled=True)
        return lax.all_gather(packed, COL_PARTS[:2], axis=0, tiled=True)
    return lax.all_gather(packed, "col", axis=0, tiled=True)


def body(flow_cols, flow_vals, window_flow, split):
    row = lax.axis_index("row")
    layer = lax.axis_index("layer")
    n_layer = lax.axis_size("layer")
    own_g = window_flow[0]
    half_rows = own_g.shape[0]
    other_g = lax.ppermute(own_g, "row", perm=[(0, 1), (1, 0)])
    panel = jnp.zeros((2 * half_rows, own_g.shape[1]), own_g.dtype)
    panel = lax.dynamic_update_slice_in_dim(panel, own_g, row * half_rows, 0)
    panel = lax.dynamic_update_slice_in_dim(panel, other_g, (1 - row) * half_rows, 0)

    block_size = flow_vals.shape[-1]
    block_count = panel.shape[0] // block_size
    row_blocks = flow_vals.shape[0]
    stacked = flow_vals.reshape(1, row_blocks * block_size, block_size)
    col_tile = jnp.zeros((1, 16, block_size), jnp.bfloat16)
    col_tile = col_tile.at[0, 0, :row_blocks].set(flow_cols.reshape(row_blocks).astype(jnp.bfloat16))
    packed = jnp.concatenate([stacked, col_tile], axis=1)
    gathered = gather_slots(packed, split)
    slot_cols = gathered[:, row_blocks * block_size, :row_blocks].astype(jnp.int32).T
    slot_count = gathered.shape[0]
    hit = slot_cols[:, :, None] == jnp.arange(block_count, dtype=jnp.int32)[None, None, :]
    slot_ids = jnp.arange(slot_count, dtype=jnp.int32)[None, :, None]
    slot_of = jnp.max(jnp.where(hit, slot_ids, -1), axis=1)

    share = row_blocks // n_layer
    send_first = ((1 - layer) * share).astype(jnp.int32).reshape(1)
    keep_first = (layer * share).astype(jnp.int32).reshape(1)

    def expand(first):
        return dense_rows(first, slot_of, gathered, panel, share)

    received = []
    for part in range(2):
        sent = dense_rows(send_first, slot_of, gathered, panel, share, col_parts=2, col_part=part, group=share // 2)
        received.append(lax.ppermute(sent, "layer", perm=[(0, 1), (1, 0)]))
    summed = expand(keep_first) + jnp.concatenate(received, axis=1)
    squares = summed * summed
    total_rows = row_blocks * block_size * lax.axis_size("row")
    column_sums = jnp.sum(squares, axis=0)
    for axis in ("row", "layer"):
        column_sums = column_sums + lax.ppermute(column_sums, axis, perm=[(0, 1), (1, 0)])
    return squares / (column_sums / total_rows + 1e-06)


def solution(mesh):
    split = mesh.shape["col"] == COL_FACTORS[0] * COL_FACTORS[1] * COL_FACTORS[2]
    if split:
        devices = mesh.devices.reshape(
            (mesh.shape["row"],) + COL_FACTORS + (mesh.shape["layer"],)
        )
        mesh = Mesh(devices, ("row",) + COL_PARTS + ("layer",))
        col = COL_PARTS
    else:
        col = "col"
    placed = (
        P("row", "layer", col),
        P("row", "layer", col, None, None),
        P("layer", "row", col),
    )
    return jax.shard_map(
        lambda c, v, w: body(c, v, w, split),
        mesh=mesh, in_specs=placed, out_specs=P(("row", "layer"), col), check_vma=False,
    )
```

```python
import jax
import jax.numpy as jnp
from jax.experimental import pallas as pl
from jax.experimental.pallas import tpu as pltpu
from jax import lax
from jax.sharding import Mesh, PartitionSpec as P


def dense_rows_kernel(first_ref, slot_of_ref, vals_ref, panel_ref, out_ref, stage_ref):
    block_size = vals_ref.shape[-1]
    share = vals_ref.shape[1] // block_size
    width = stage_ref.shape[1] // block_size
    j = pl.program_id(0)
    first = first_ref[0]

    @pl.when(j == 0)
    def _():
        out_ref[...] = jnp.zeros_like(out_ref)

    for i in range(share):
        for kk in range(width):
            slot = slot_of_ref[first + i, j * width + kk]
            rows = pl.ds(i * block_size, block_size)
            block = vals_ref[jnp.maximum(slot, 0), rows, :]
            stage_ref[rows, pl.ds(kk * block_size, block_size)] = jnp.where(
                slot >= 0, block, jnp.zeros_like(block)
            )

    out_ref[...] += jnp.dot(stage_ref[...], panel_ref[...], preferred_element_type=jnp.float32)


def dense_rows(first, slot_of, gathered, panel, share, width=32, col_parts=1, col_part=0):
    slot_count = gathered.shape[0]
    block_size = gathered.shape[-1]
    out_cols = panel.shape[1] // col_parts
    return pl.pallas_call(
        dense_rows_kernel,
        out_shape=jax.ShapeDtypeStruct((share * block_size, out_cols), jnp.float32),
        grid_spec=pltpu.PrefetchScalarGridSpec(
            num_scalar_prefetch=2,
            grid=(panel.shape[0] // (width * block_size),),
            in_specs=[
                pl.BlockSpec((slot_count, share * block_size, block_size),
                             lambda j, f, t: (0, f[0] // share, 0), pipeline_mode=pl.Buffered(1)),
                pl.BlockSpec((width * block_size, out_cols), lambda j, f, t: (j, col_part)),
            ],
            out_specs=pl.BlockSpec((share * block_size, out_cols), lambda j, f, t: (0, 0)),
            scratch_shapes=[pltpu.VMEM((share * block_size, width * block_size), jnp.bfloat16)],
        ),
        compiler_params=pltpu.CompilerParams(vmem_limit_bytes=48 * 1024 * 1024),
        cost_estimate=pl.CostEstimate(
            flops=2 * share * block_size * panel.shape[0] * out_cols,
            transcendentals=0,
            bytes_accessed=slot_count * share * block_size * block_size * 2 + panel.size * 2 // col_parts + share * block_size * out_cols * 4,
        ),
    )(first, slot_of, gathered, panel)


COL_FACTORS = (8, 4, 2)
COL_PARTS = ("col_z", "col_y", "col_x")


def gather_slots(packed, split):
    if split:
        packed = lax.all_gather(packed, COL_PARTS[2], axis=0, tiled=True)
        return lax.all_gather(packed, COL_PARTS[:2], axis=0, tiled=True)
    return lax.all_gather(packed, "col", axis=0, tiled=True)


def body(flow_cols, flow_vals, window_flow, split):
    row = lax.axis_index("row")
    layer = lax.axis_index("layer")
    n_layer = lax.axis_size("layer")
    own_g = window_flow[0]
    half_rows = own_g.shape[0]
    other_g = lax.ppermute(own_g, "row", perm=[(0, 1), (1, 0)])
    panel = jnp.zeros((2 * half_rows, own_g.shape[1]), own_g.dtype)
    panel = lax.dynamic_update_slice_in_dim(panel, own_g, row * half_rows, 0)
    panel = lax.dynamic_update_slice_in_dim(panel, other_g, (1 - row) * half_rows, 0)

    block_size = flow_vals.shape[-1]
    block_count = panel.shape[0] // block_size
    row_blocks = flow_vals.shape[0]
    stacked = flow_vals.reshape(1, row_blocks * block_size, block_size)
    col_tile = jnp.zeros((1, 16, block_size), jnp.bfloat16)
    col_tile = col_tile.at[0, 0, :row_blocks].set(flow_cols.reshape(row_blocks).astype(jnp.bfloat16))
    packed = jnp.concatenate([stacked, col_tile], axis=1)
    gathered = gather_slots(packed, split)
    slot_cols = gathered[:, row_blocks * block_size, :row_blocks].astype(jnp.int32).T
    slot_count = gathered.shape[0]
    hit = slot_cols[:, :, None] == jnp.arange(block_count, dtype=jnp.int32)[None, None, :]
    slot_ids = jnp.arange(slot_count, dtype=jnp.int32)[None, :, None]
    slot_of = jnp.max(jnp.where(hit, slot_ids, -1), axis=1)

    share = row_blocks // n_layer
    send_first = ((1 - layer) * share).astype(jnp.int32).reshape(1)
    keep_first = (layer * share).astype(jnp.int32).reshape(1)

    def expand(first):
        return dense_rows(first, slot_of, gathered, panel, share)

    received = []
    half = share // 2
    for part in range(2):
        sent = dense_rows(send_first + part * half, slot_of, gathered, panel, half)
        received.append(lax.ppermute(sent, "layer", perm=[(0, 1), (1, 0)]))
    summed = expand(keep_first) + jnp.concatenate(received, axis=0)
    squares = summed * summed
    total_rows = row_blocks * block_size * lax.axis_size("row")
    column_sums = jnp.sum(squares, axis=0)
    for axis in ("row", "layer"):
        column_sums = column_sums + lax.ppermute(column_sums, axis, perm=[(0, 1), (1, 0)])
    return squares / (column_sums / total_rows + 1e-06)


def solution(mesh):
    split = mesh.shape["col"] == COL_FACTORS[0] * COL_FACTORS[1] * COL_FACTORS[2]
    if split:
        devices = mesh.devices.reshape(
            (mesh.shape["row"],) + COL_FACTORS + (mesh.shape["layer"],)
        )
        mesh = Mesh(devices, ("row",) + COL_PARTS + ("layer",))
        col = COL_PARTS
    else:
        col = "col"
    placed = (
        P("row", "layer", col),
        P("row", "layer", col, None, None),
        P("layer", "row", col),
    )
    return jax.shard_map(
        lambda c, v, w: body(c, v, w, split),
        mesh=mesh, in_specs=placed, out_specs=P(("row", "layer"), col), check_vma=False,
    )
```

```python
import jax
import jax.numpy as jnp
from jax.experimental import pallas as pl
from jax.experimental.pallas import tpu as pltpu
from jax import lax
from jax.sharding import Mesh, PartitionSpec as P


def dense_rows_kernel(first_ref, slot_of_ref, vals_ref, panel_ref, out_ref, stage_ref):
    block_size = vals_ref.shape[-1]
    share = vals_ref.shape[1] // block_size
    width = stage_ref.shape[1] // block_size
    j = pl.program_id(0)
    first = first_ref[0]

    @pl.when(j == 0)
    def _():
        out_ref[...] = jnp.zeros_like(out_ref)

    for i in range(share):
        for kk in range(width):
            slot = slot_of_ref[first + i, j * width + kk]
            rows = pl.ds(i * block_size, block_size)
            block = vals_ref[jnp.maximum(slot, 0), rows, :]
            stage_ref[rows, pl.ds(kk * block_size, block_size)] = jnp.where(
                slot >= 0, block, jnp.zeros_like(block)
            )

    out_ref[...] += jnp.dot(stage_ref[...], panel_ref[...], preferred_element_type=jnp.float32)


def dense_rows(first, slot_of, gathered, panel, share, width=32, col_parts=1, col_part=0):
    slot_count = gathered.shape[0]
    block_size = gathered.shape[-1]
    out_cols = panel.shape[1] // col_parts
    return pl.pallas_call(
        dense_rows_kernel,
        out_shape=jax.ShapeDtypeStruct((share * block_size, out_cols), jnp.float32),
        grid_spec=pltpu.PrefetchScalarGridSpec(
            num_scalar_prefetch=2,
            grid=(panel.shape[0] // (width * block_size),),
            in_specs=[
                pl.BlockSpec((slot_count, share * block_size, block_size),
                             lambda j, f, t: (0, f[0] // share, 0), pipeline_mode=pl.Buffered(1)),
                pl.BlockSpec((width * block_size, out_cols), lambda j, f, t: (j, col_part)),
            ],
            out_specs=pl.BlockSpec((share * block_size, out_cols), lambda j, f, t: (0, 0)),
            scratch_shapes=[pltpu.VMEM((share * block_size, width * block_size), jnp.bfloat16)],
        ),
        compiler_params=pltpu.CompilerParams(vmem_limit_bytes=48 * 1024 * 1024),
        cost_estimate=pl.CostEstimate(
            flops=2 * share * block_size * panel.shape[0] * out_cols,
            transcendentals=0,
            bytes_accessed=slot_count * share * block_size * block_size * 2 + panel.size * 2 // col_parts + share * block_size * out_cols * 4,
        ),
    )(first, slot_of, gathered, panel)


COL_FACTORS = (8, 4, 2)
COL_PARTS = ("col_z", "col_y", "col_x")


def gather_slots(packed, split):
    if split:
        packed = lax.all_gather(packed, COL_PARTS[2], axis=0, tiled=True)
        return lax.all_gather(packed, COL_PARTS[:2], axis=0, tiled=True)
    return lax.all_gather(packed, "col", axis=0, tiled=True)


def body(flow_cols, flow_vals, window_flow, split):
    row = lax.axis_index("row")
    layer = lax.axis_index("layer")
    n_layer = lax.axis_size("layer")
    own_g = window_flow[0]
    half_rows = own_g.shape[0]
    other_g = lax.ppermute(own_g, "row", perm=[(0, 1), (1, 0)])
    panel = jnp.zeros((2 * half_rows, own_g.shape[1]), own_g.dtype)
    panel = lax.dynamic_update_slice_in_dim(panel, own_g, row * half_rows, 0)
    panel = lax.dynamic_update_slice_in_dim(panel, other_g, (1 - row) * half_rows, 0)

    block_size = flow_vals.shape[-1]
    block_count = panel.shape[0] // block_size
    row_blocks = flow_vals.shape[0]
    stacked = flow_vals.reshape(1, row_blocks * block_size, block_size)
    col_tile = jnp.zeros((1, 16, block_size), jnp.bfloat16)
    col_tile = col_tile.at[0, 0, :row_blocks].set(flow_cols.reshape(row_blocks).astype(jnp.bfloat16))
    packed = jnp.concatenate([stacked, col_tile], axis=1)
    gathered = gather_slots(packed, split)
    slot_cols = gathered[:, row_blocks * block_size, :row_blocks].astype(jnp.int32).T
    slot_count = gathered.shape[0]
    hit = slot_cols[:, :, None] == jnp.arange(block_count, dtype=jnp.int32)[None, None, :]
    slot_ids = jnp.arange(slot_count, dtype=jnp.int32)[None, :, None]
    slot_of = jnp.max(jnp.where(hit, slot_ids, -1), axis=1)

    share = row_blocks // n_layer
    send_first = ((1 - layer) * share).astype(jnp.int32).reshape(1)
    keep_first = (layer * share).astype(jnp.int32).reshape(1)

    def expand(first):
        return dense_rows(first, slot_of, gathered, panel, share)

    received = []
    half = share // 2
    for part in range(2):
        sent = dense_rows(send_first + part * half, slot_of, gathered, panel, half, width=16)
        received.append(lax.ppermute(sent, "layer", perm=[(0, 1), (1, 0)]))
    summed = expand(keep_first) + jnp.concatenate(received, axis=0)
    squares = summed * summed
    total_rows = row_blocks * block_size * lax.axis_size("row")
    column_sums = jnp.sum(squares, axis=0)
    for axis in ("row", "layer"):
        column_sums = column_sums + lax.ppermute(column_sums, axis, perm=[(0, 1), (1, 0)])
    return squares / (column_sums / total_rows + 1e-06)


def solution(mesh):
    split = mesh.shape["col"] == COL_FACTORS[0] * COL_FACTORS[1] * COL_FACTORS[2]
    if split:
        devices = mesh.devices.reshape(
            (mesh.shape["row"],) + COL_FACTORS + (mesh.shape["layer"],)
        )
        mesh = Mesh(devices, ("row",) + COL_PARTS + ("layer",))
        col = COL_PARTS
    else:
        col = "col"
    placed = (
        P("row", "layer", col),
        P("row", "layer", col, None, None),
        P("layer", "row", col),
    )
    return jax.shard_map(
        lambda c, v, w: body(c, v, w, split),
        mesh=mesh, in_specs=placed, out_specs=P(("row", "layer"), col), check_vma=False,
    )
```

```python
import jax
import jax.numpy as jnp
from jax.experimental import pallas as pl
from jax.experimental.pallas import tpu as pltpu
from jax import lax
from jax.sharding import Mesh, PartitionSpec as P


def dense_rows_kernel(first_ref, slot_of_ref, vals_ref, panel_ref, out_ref, stage_ref):
    block_size = vals_ref.shape[-1]
    share = vals_ref.shape[1] // block_size
    width = stage_ref.shape[1] // block_size
    j = pl.program_id(0)
    first = first_ref[0]

    @pl.when(j == 0)
    def _():
        out_ref[...] = jnp.zeros_like(out_ref)

    for i in range(share):
        for kk in range(width):
            slot = slot_of_ref[first + i, j * width + kk]
            rows = pl.ds(i * block_size, block_size)
            block = vals_ref[jnp.maximum(slot, 0), rows, :]
            stage_ref[rows, pl.ds(kk * block_size, block_size)] = jnp.where(
                slot >= 0, block, jnp.zeros_like(block)
            )

    out_ref[...] += jnp.dot(stage_ref[...], panel_ref[...], preferred_element_type=jnp.float32)


def dense_rows(first, slot_of, gathered, panel, share, width=32, col_parts=1, col_part=0):
    slot_count = gathered.shape[0]
    block_size = gathered.shape[-1]
    out_cols = panel.shape[1] // col_parts
    return pl.pallas_call(
        dense_rows_kernel,
        out_shape=jax.ShapeDtypeStruct((share * block_size, out_cols), jnp.float32),
        grid_spec=pltpu.PrefetchScalarGridSpec(
            num_scalar_prefetch=2,
            grid=(panel.shape[0] // (width * block_size),),
            in_specs=[
                pl.BlockSpec((slot_count, share * block_size, block_size),
                             lambda j, f, t: (0, f[0] // share, 0), pipeline_mode=pl.Buffered(1)),
                pl.BlockSpec((width * block_size, out_cols), lambda j, f, t: (j, col_part)),
            ],
            out_specs=pl.BlockSpec((share * block_size, out_cols), lambda j, f, t: (0, 0)),
            scratch_shapes=[pltpu.VMEM((share * block_size, width * block_size), jnp.bfloat16)],
        ),
        compiler_params=pltpu.CompilerParams(vmem_limit_bytes=48 * 1024 * 1024),
        cost_estimate=pl.CostEstimate(
            flops=2 * share * block_size * panel.shape[0] * out_cols,
            transcendentals=0,
            bytes_accessed=slot_count * share * block_size * block_size * 2 + panel.size * 2 // col_parts + share * block_size * out_cols * 4,
        ),
    )(first, slot_of, gathered, panel)


COL_FACTORS = (8, 4, 2)
COL_PARTS = ("col_z", "col_y", "col_x")


def gather_slots(stacked, col_tile, split):
    packed = jnp.concatenate([stacked, col_tile], axis=1)
    if split:
        swap = [(0, 1), (1, 0)]
        partner = jnp.concatenate(
            [lax.ppermute(stacked, COL_PARTS[2], swap), lax.ppermute(col_tile, COL_PARTS[2], swap)], axis=1
        )
        packed = jnp.concatenate([packed, partner], axis=0)
        return lax.all_gather(packed, COL_PARTS[:2], axis=0, tiled=True)
    return lax.all_gather(packed, "col", axis=0, tiled=True)


def body(flow_cols, flow_vals, window_flow, split):
    row = lax.axis_index("row")
    layer = lax.axis_index("layer")
    n_layer = lax.axis_size("layer")
    own_g = window_flow[0]
    half_rows = own_g.shape[0]
    other_g = lax.ppermute(own_g, "row", perm=[(0, 1), (1, 0)])
    panel = jnp.zeros((2 * half_rows, own_g.shape[1]), own_g.dtype)
    panel = lax.dynamic_update_slice_in_dim(panel, own_g, row * half_rows, 0)
    panel = lax.dynamic_update_slice_in_dim(panel, other_g, (1 - row) * half_rows, 0)

    block_size = flow_vals.shape[-1]
    block_count = panel.shape[0] // block_size
    row_blocks = flow_vals.shape[0]
    stacked = flow_vals.reshape(1, row_blocks * block_size, block_size)
    col_tile = jnp.zeros((1, 16, block_size), jnp.bfloat16)
    col_tile = col_tile.at[0, 0, :row_blocks].set(flow_cols.reshape(row_blocks).astype(jnp.bfloat16))
    gathered = gather_slots(stacked, col_tile, split)
    slot_cols = gathered[:, row_blocks * block_size, :row_blocks].astype(jnp.int32).T
    slot_count = gathered.shape[0]
    hit = slot_cols[:, :, None] == jnp.arange(block_count, dtype=jnp.int32)[None, None, :]
    slot_ids = jnp.arange(slot_count, dtype=jnp.int32)[None, :, None]
    slot_of = jnp.max(jnp.where(hit, slot_ids, -1), axis=1)

    share = row_blocks // n_layer
    send_first = ((1 - layer) * share).astype(jnp.int32).reshape(1)
    keep_first = (layer * share).astype(jnp.int32).reshape(1)

    def expand(first):
        return dense_rows(first, slot_of, gathered, panel, share)

    received = []
    half = share // 2
    for part in range(2):
        sent = dense_rows(send_first + part * half, slot_of, gathered, panel, half)
        received.append(lax.ppermute(sent, "layer", perm=[(0, 1), (1, 0)]))
    summed = expand(keep_first) + jnp.concatenate(received, axis=0)
    squares = summed * summed
    total_rows = row_blocks * block_size * lax.axis_size("row")
    column_sums = jnp.sum(squares, axis=0)
    for axis in ("row", "layer"):
        column_sums = column_sums + lax.ppermute(column_sums, axis, perm=[(0, 1), (1, 0)])
    return squares / (column_sums / total_rows + 1e-06)


def solution(mesh):
    split = mesh.shape["col"] == COL_FACTORS[0] * COL_FACTORS[1] * COL_FACTORS[2]
    if split:
        devices = mesh.devices.reshape(
            (mesh.shape["row"],) + COL_FACTORS + (mesh.shape["layer"],)
        )
        mesh = Mesh(devices, ("row",) + COL_PARTS + ("layer",))
        col = COL_PARTS
    else:
        col = "col"
    placed = (
        P("row", "layer", col),
        P("row", "layer", col, None, None),
        P("layer", "row", col),
    )
    return jax.shard_map(
        lambda c, v, w: body(c, v, w, split),
        mesh=mesh, in_specs=placed, out_specs=P(("row", "layer"), col), check_vma=False,
    )
```
